32 devices in a mesh: grp: 2 (over y), col: 4 (over z), freq: 2 (over x), rep: 2 (over core).
Axes of the slice: x: 2, y: 2, z: 4, core: 2. Of those that a mesh axis runs over, the one named last changes fastest.
Arguments:
- focusing: float32 [2, 2, 512, 16384], P('freq', None, ('grp', 'rep'), 'col'), parts along dimension 2, may hold values from -6 to 6
- v_factors: bfloat16 [2, 2, 384, 16384], P('freq', None, None, 'col'), may hold values from -0.1875 to 0.1875
- u_factors: bfloat16 [2, 2, 16, 384, 1024], P('freq', None, 'col'), may hold values from -0.3125 to 0.3125
- tile_ranks: int32 [16, 16], replicated, may hold values from 1 to 24
- owners: int32 [16], replicated, may hold values from 0 to 3, as said below
- onsets: int32 [16384], replicated, may hold values from 64 to 511
Outputs:
- update: float32 [2, 2, 512, 16384], P('freq', None, ('grp', 'rep'), 'col'), parts along dimension 2
The draws below stay inside these ranges and needn't reach their ends.
There are 2 independent parts, one for each index of `grp`. The reference program is written for one: setup_inputs(seed, part) draws one part's arguments, and reference() takes and returns one part's arrays. A program takes and returns all parts, laid end to end along the dimension named above; an argument that names none is the same for every part. Nothing has to cross between parts.
Inputs may be any that keep to these rules, and one draw needn't show every extreme that they name: `owners`: no owner holds more than 4 row tiles, and some owner holds exactly 4; the factors of row tile I stand in slot slot[I] of u_factors as the steps define it.
All inputs are finite; a program needn't handle non-finite values.
Results may differ from the reference program's by a relative error of at most 0.0062.
Values may be sent and summed in bfloat16 or wider, within the bound.
A program may use at most 64 MiB of HBM per device.

```python
import jax
import jax.numpy as jnp
from jax import lax

TS = 1024
R = 24
NR = 16384
NS = 16384
NT = 512
KLO = 8
NF = 2
NV = 256
NRT = 16
NST = 16
BW = 1024
CAP = 4
SLOTS = 16


def draw_owners(key, part):
    key_order, key_rest, key_tiles = jax.random.split(jax.random.fold_in(key, 11), 3)
    owner_count = SLOTS // CAP
    order = jax.random.permutation(key_order, owner_count).astype(jnp.int32)
    others = jax.random.permutation(key_rest, SLOTS - CAP)[:NRT - CAP].astype(jnp.int32)
    first = jnp.full((CAP,), order[0], jnp.int32)
    remaining = order[1 + others // CAP]
    listed = jnp.concatenate([first, remaining]).astype(jnp.int32)
    tile_order = jax.random.permutation(key_tiles, NRT).astype(jnp.int32)
    return jnp.zeros((NRT,), jnp.int32).at[tile_order].set(listed)


def set_ends(array, key, least, largest):
    index_at = [jax.random.randint(jax.random.fold_in(key, axis), (), 0, length) for axis, length in enumerate(array.shape)]
    widest = array.shape.index(max(array.shape))
    neighbour = index_at[:widest] + [(index_at[widest] + 1) % array.shape[widest]] + index_at[widest + 1:]
    return array.at[tuple(index_at)].set(least).at[tuple(neighbour)].set(largest)


def block_scale(own_key, dims, cuts, least, largest):
    level = 1.0
    for dim, shards_of in cuts:
        steps = jax.random.uniform(jax.random.fold_in(jax.random.fold_in(own_key, 6), dim), (shards_of,), jnp.float32, least / len(cuts), largest / len(cuts))
        level = level * jnp.repeat(jnp.exp(steps), dims[dim] // shards_of).reshape((-1,) + (1,) * (len(dims) - 1 - dim))
    return level


def normal_values(stream_key, extent, scale, most, cuts=(), held_as=jnp.bfloat16):
    entries = jax.random.normal(stream_key, extent, jnp.float32) * scale
    if len(cuts) > 0:
        entries = block_scale(stream_key, extent, cuts, -0.22, 0.18) * entries
    return jnp.clip(entries, min=-most, max=most).astype(held_as)


def setup_inputs(seed: int = 0, part: int = 0) -> dict:
    key_list = jax.random.split(jax.random.key(seed), 7)
    part_splits = jax.random.split(jax.random.fold_in(key_list[6], part), 7)
    focusing = normal_values(part_splits[0], (NF, 2, NV, NS), 1.0, 6.0, ((0, 2), (2, 2), (3, 4)), jnp.float32)
    v_factors = normal_values(key_list[1], (NF, 2, NRT * R, NS), TS ** -0.5, 0.1875, ((0, 2), (3, 4)))
    u_factors = normal_values(key_list[2], (NF, 2, SLOTS, NST * R, TS), (NST * R) ** -0.5, 0.3125, ((0, 2), (2, 4)))
    tile_ranks = set_ends(jax.random.randint(key_list[3], (NRT, NST), 1, R + 1), jax.random.fold_in(key_list[3], 1), 1, R).astype(jnp.int32)
    owners = draw_owners(jax.random.fold_in(key_list[6], 71), part)
    onsets = set_ends(jax.random.randint(key_list[5], (NR,), NT // 8, NT), jax.random.fold_in(key_list[5], 1), NT // 8, NT - 1).astype(jnp.int32)
    return {"focusing": focusing, "v_factors": v_factors, "u_factors": u_factors, "tile_ranks": tile_ranks, "owners": owners, "onsets": onsets}


def window_tables(count_freq, onset_rows):
    time_steps = jnp.arange(NT, dtype=jnp.int32)
    freq_bins = KLO + jnp.arange(count_freq, dtype=jnp.int32)
    phases = 2.0 * jnp.pi * ((freq_bins[None, :] * time_steps[:, None]) % NT).astype(jnp.float32) / NT
    cosine = jnp.cos(phases)
    sines = jnp.sin(phases)
    analyse = jnp.stack([cosine, -sines], axis=2).reshape(NT, 2 * count_freq)
    synthesis = analyse * (2.0 / NT)
    product_table = (analyse[:, :, None] * synthesis[:, None, :]).reshape(NT, 4 * count_freq * count_freq)
    running_table = jnp.cumsum(product_table, axis=0)
    mixing = jnp.take(running_table, (onset_rows - 1).astype(jnp.int32), axis=0)
    return mixing.reshape(-1, 2 * count_freq, 2 * count_freq)


def settle(values):
    return lax.optimization_barrier(values.astype(jnp.bfloat16)).astype(jnp.float32)


def kernel_product(einsum_recipe, left_side, right_side):
    return jnp.einsum(einsum_recipe, left_side, right_side, precision=lax.Precision.HIGHEST)


def reference(focusing, v_factors, u_factors, tile_ranks, owners, onsets):
    row_tiles = NR // TS
    col_tiles = NS // TS
    all_blocks = NS // BW
    per_tile = TS // BW
    focus_low = settle(focusing).reshape(NF, 2, NV, all_blocks, BW)
    factors_v = v_factors.astype(jnp.float32).reshape(NF, 2, row_tiles, R, all_blocks, BW)
    einsum_recipe = "fikbs,fvbs->ifbkv"
    real_portion = kernel_product(einsum_recipe, factors_v[:, 0], focus_low[:, 0]) - kernel_product(einsum_recipe, factors_v[:, 1], focus_low[:, 1])
    part_imag = kernel_product(einsum_recipe, factors_v[:, 0], focus_low[:, 1]) + kernel_product(einsum_recipe, factors_v[:, 1], focus_low[:, 0])
    partial_sums = settle(jnp.stack([real_portion, part_imag], axis=3))
    coefficients = jnp.sum(partial_sums.reshape(row_tiles, NF, col_tiles, per_tile, 2, R, NV), axis=3)
    rank_mask = (jnp.arange(R, dtype=jnp.int32)[None, None, :] < tile_ranks[:, :, None]).astype(jnp.float32)
    coefficients = settle(coefficients * rank_mask[:, None, :, None, :, None])
    tile_ids = jnp.arange(row_tiles, dtype=jnp.int32)
    same_owner = owners[:, None] == owners[None, :]
    earlier = tile_ids[None, :] < tile_ids[:, None]
    slot_of = jnp.sum((same_owner & earlier).astype(jnp.int32), axis=1)
    destination = (owners * CAP + slot_of).astype(jnp.int32)
    chosen = jnp.take(u_factors, destination, axis=2).astype(jnp.float32)
    chosen = chosen.reshape(NF, 2, row_tiles, col_tiles, R, TS)
    uform = "fijka,ifjkv->ifav"
    field_real = kernel_product(uform, chosen[:, 0], coefficients[:, :, :, 0]) - kernel_product(uform, chosen[:, 1], coefficients[:, :, :, 1])
    field_imag = kernel_product(uform, chosen[:, 0], coefficients[:, :, :, 1]) + kernel_product(uform, chosen[:, 1], coefficients[:, :, :, 0])
    receiver_field = settle(jnp.stack([field_real, field_imag], axis=2))
    mixing = window_tables(NF, onsets).reshape(row_tiles, TS, 2 * NF, 2 * NF)
    flat_field = receiver_field.reshape(row_tiles, 2 * NF, TS, NV)
    windowed = settle(kernel_product("itpq,iqtv->iptv", mixing, flat_field)).reshape(row_tiles, NF, 2, TS, NV)
    aform = "fijka,ifav->ifjkv"
    back_real = kernel_product(aform, chosen[:, 0], windowed[:, :, 0]) + kernel_product(aform, chosen[:, 1], windowed[:, :, 1])
    back_imag = kernel_product(aform, chosen[:, 0], windowed[:, :, 1]) - kernel_product(aform, chosen[:, 1], windowed[:, :, 0])
    adjoint = jnp.stack([back_real, back_imag], axis=3) * rank_mask[:, None, :, None, :, None]
    adjoint = settle(adjoint)
    spread = jnp.broadcast_to(adjoint[:, :, :, None], (row_tiles, NF, col_tiles, per_tile, 2, R, NV))
    spread = spread.reshape(row_tiles, NF, all_blocks, 2, R, NV)
    wform = "fikbs,ifbkv->fvbs"
    wave_real = kernel_product(wform, factors_v[:, 0], spread[:, :, :, 0]) + kernel_product(wform, factors_v[:, 1], spread[:, :, :, 1])
    wave_imag = kernel_product(wform, factors_v[:, 0], spread[:, :, :, 1]) - kernel_product(wform, factors_v[:, 1], spread[:, :, :, 0])
    wave_field = jnp.stack([wave_real, wave_imag], axis=1).reshape(NF, 2, NV, NS)
    return focusing - wave_field
```

```python
import functools
import math

import jax
import jax.numpy as jnp
from jax import lax
from jax.experimental import pallas as pl
from jax.experimental.pallas import tpu as pltpu
from jax.sharding import PartitionSpec as P

TS = 1024
R = 24
NR = 16384
NS = 16384
NT = 512
KLO = 8
LANES = 128
ROUNDS = 2
CHUNKS = 3


def window_tables(count_freq, onset_rows):
    time_steps = jnp.arange(NT, dtype=jnp.int32)
    freq_bins = KLO + jnp.arange(count_freq, dtype=jnp.int32)
    phases = 2.0 * jnp.pi * (freq_bins[None, :] * time_steps[:, None] % NT).astype(jnp.float32) / NT
    cosine = jnp.cos(phases)
    sines = jnp.sin(phases)
    analyse = jnp.stack([cosine, -sines], axis=2).reshape(NT, 2 * count_freq)
    synthesis = analyse * (2.0 / NT)
    product_table = (analyse[:, :, None] * synthesis[:, None, :]).reshape(
        NT, 4 * count_freq * count_freq
    )
    lower = (time_steps[:, None] >= time_steps[None, :]).astype(jnp.float32)
    running_table = jnp.dot(lower, product_table, precision=lax.Precision.HIGHEST)
    mixing = jnp.take(running_table, onset_rows - 1, axis=0)
    return mixing.reshape(-1, 2 * count_freq, 2 * count_freq)


def kernel_product(einsum_recipe, left_side, right_side):
    return jnp.einsum(einsum_recipe, left_side, right_side, preferred_element_type=jnp.float32)


def per_device(focusing, v_factors, u_factors, tile_ranks, owners, onsets):
    count_col = lax.axis_size("col")
    my_column = lax.axis_index("col")
    count_freq = lax.axis_size("freq")
    my_freq = lax.axis_index("freq")
    freq_dev = focusing.shape[0]
    vis_dev = focusing.shape[2]
    sources_dev = focusing.shape[3]
    capacity = u_factors.shape[2]
    block_width = min(sources_dev, TS)
    blocks_dev = sources_dev // block_width
    per_tile = TS // block_width
    all_blocks = count_col * blocks_dev
    row_tiles = NR // TS
    col_tiles = NS // TS
    freq_all = freq_dev * count_freq
    quarter = TS // count_freq
    tile_ids = jnp.arange(row_tiles, dtype=jnp.int32)
    same_owner = owners[:, None] == owners[None, :]
    earlier = tile_ids[None, :] < tile_ids[:, None]
    slot_of = jnp.sum((same_owner & earlier).astype(jnp.int32), axis=1)
    slot_ids = jnp.arange(capacity, dtype=jnp.int32)
    routing = (owners[None, None, :] == jnp.arange(count_col, dtype=jnp.int32)[:, None, None]) & (
        slot_of[None, None, :] == slot_ids[None, :, None]
    )
    lower_routing = routing.astype(jnp.bfloat16)
    my_slots = ((owners[None, :] == my_column) & (slot_of[None, :] == slot_ids[:, None])).astype(
        jnp.int32
    )
    slot_ranks = jnp.sum(my_slots[:, :, None] * tile_ranks[None, :, :], axis=1)
    rank_mask = (jnp.arange(R, dtype=jnp.int32)[None, None, :] < slot_ranks[:, :, None]).astype(
        jnp.float32
    )
    slot_onsets = jnp.sum(my_slots[:, :, None] * onsets.reshape(row_tiles, TS)[None], axis=1)
    slot_onsets = jnp.maximum(slot_onsets, 1)
    focus_low = focusing.astype(jnp.bfloat16).reshape(freq_dev, 2, vis_dev, blocks_dev, block_width)
    factors_v = v_factors.reshape(freq_dev, 2, row_tiles, R, blocks_dev, block_width)
    einsum_recipe = "fikbs,fvbs->ifbkv"
    real_portion = kernel_product(einsum_recipe, factors_v[:, 0], focus_low[:, 0]) - kernel_product(
        einsum_recipe, factors_v[:, 1], focus_low[:, 1]
    )
    part_imag = kernel_product(einsum_recipe, factors_v[:, 0], focus_low[:, 1]) + kernel_product(
        einsum_recipe, factors_v[:, 1], focus_low[:, 0]
    )
    partial_sums = jnp.stack([real_portion, part_imag], axis=3).astype(jnp.bfloat16)
    outgoing_parts = kernel_product("way,ymleno->amwleno", lower_routing, partial_sums).astype(
        jnp.bfloat16
    )
    outgoing_parts = outgoing_parts.reshape(capacity, freq_dev, all_blocks, 2, R, vis_dev)
    arrived = lax.all_to_all(outgoing_parts, "col", split_axis=2, concat_axis=2, tiled=True)
    coefficients = jnp.sum(
        arrived.astype(jnp.float32).reshape(capacity, freq_dev, col_tiles, per_tile, 2, R, vis_dev),
        axis=3,
    )
    coefficients = (coefficients * rank_mask[:, None, :, None, :, None]).astype(jnp.bfloat16)
    factors_u = u_factors.reshape(freq_dev, 2, capacity, col_tiles, R, TS)
    uform = "fcjka,cfjkv->cfav"
    field_real = kernel_product(uform, factors_u[:, 0], coefficients[:, :, :, 0]) - kernel_product(
        uform, factors_u[:, 1], coefficients[:, :, :, 1]
    )
    field_imag = kernel_product(uform, factors_u[:, 0], coefficients[:, :, :, 1]) + kernel_product(
        uform, factors_u[:, 1], coefficients[:, :, :, 0]
    )
    receiver_field = jnp.stack([field_real, field_imag], axis=2).astype(jnp.bfloat16)
    turned = lax.all_to_all(receiver_field, "freq", split_axis=3, concat_axis=1, tiled=True)
    quarter_onsets = lax.dynamic_slice_in_dim(slot_onsets, my_freq * quarter, quarter, 1)
    mixing = window_tables(freq_all, quarter_onsets.reshape(-1)).reshape(
        capacity, quarter, 2 * freq_all, 2 * freq_all
    )
    flat_field = turned.reshape(capacity, 2 * freq_all, quarter, vis_dev).astype(jnp.float32)
    mixed_field = jnp.einsum("crpq,cqrv->cprv", mixing, flat_field, precision=lax.Precision.HIGHEST)
    mixed_field = mixed_field.astype(jnp.bfloat16).reshape(capacity, freq_all, 2, quarter, vis_dev)
    windowed = lax.all_to_all(mixed_field, "freq", split_axis=1, concat_axis=3, tiled=True)
    aform = "fcjka,cfav->cfjkv"
    back_real = kernel_product(aform, factors_u[:, 0], windowed[:, :, 0]) + kernel_product(
        aform, factors_u[:, 1], windowed[:, :, 1]
    )
    back_imag = kernel_product(aform, factors_u[:, 0], windowed[:, :, 1]) - kernel_product(
        aform, factors_u[:, 1], windowed[:, :, 0]
    )
    adjoint = jnp.stack([back_real, back_imag], axis=3) * rank_mask[:, None, :, None, :, None]
    adjoint = adjoint.astype(jnp.bfloat16)
    spread = jnp.broadcast_to(
        adjoint[:, :, :, None], (capacity, freq_dev, col_tiles, per_tile, 2, R, vis_dev)
    )
    spread = spread.reshape(capacity, freq_dev, all_blocks, 2, R, vis_dev)
    result_field = lax.all_to_all(spread, "col", split_axis=2, concat_axis=2, tiled=True)
    result_field = result_field.reshape(capacity, freq_dev, count_col, blocks_dev, 2, R, vis_dev)
    row_share = kernel_product("prq,rjpagwu->qjagwu", lower_routing, result_field).astype(
        jnp.bfloat16
    )
    wform = "fikbs,ifbkv->fvbs"
    wave_real = kernel_product(wform, factors_v[:, 0], row_share[:, :, :, 0]) + kernel_product(
        wform, factors_v[:, 1], row_share[:, :, :, 1]
    )
    wave_imag = kernel_product(wform, factors_v[:, 0], row_share[:, :, :, 1]) - kernel_product(
        wform, factors_v[:, 1], row_share[:, :, :, 0]
    )
    wave_field = jnp.stack([wave_real, wave_imag], axis=1).reshape(
        freq_dev, 2, vis_dev, sources_dev
    )
    return focusing - wave_field


def window_rows(onset_row, my_freq):
    sign = (2 * my_freq - 1).astype(jnp.float32)

    def sums(bins, inverse):
        phase_all = jnp.bitwise_and(bins * onset_row, 2 * NT - 1).astype(jnp.float32) * (math.pi / NT)
        phase_less = jnp.bitwise_and(bins * (onset_row - 1), 2 * NT - 1).astype(jnp.float32) * (math.pi / NT)
        scaled = jnp.sin(phase_all) * inverse
        return jnp.cos(phase_less) * scaled, jnp.sin(phase_less) * scaled

    def inverse_of(bins):
        return 1.0 / (NT * math.sin(math.pi * bins / NT))

    own_inverse = jnp.where(my_freq == 0, inverse_of(2 * KLO), inverse_of(2 * KLO + 2))
    own_cos, own_sin = sums(2 * KLO + 2 * my_freq, own_inverse)
    sum_cos, sum_sin = sums(2 * KLO + 1, inverse_of(2 * KLO + 1))
    gap_cos, gap_sin = sums(1, inverse_of(1))
    level = onset_row.astype(jnp.float32) * (1.0 / NT)
    real_row = (level + own_cos, -own_sin, gap_cos + sum_cos, sign * gap_sin - sum_sin)
    imag_row = (-own_sin, level - own_cos, -sum_sin - sign * gap_sin, gap_cos - sum_cos)
    return real_row, imag_row


def stacked_dot(left_side, right_side, dims):
    return lax.dot_general(left_side, right_side, (dims, ((), ())), preferred_element_type=jnp.float32)


def fused_kernel(
    count_col,
    owners_ref,
    ranks_ref,
    onsets_ref,
    focus_hbm,
    v_hbm,
    u_hbm,
    out_ref,
    focus_buf,
    v_buf,
    v_place,
    u_buf,
    far_u,
    part_buf,
    coef_send,
    coef_recv,
    field_buf,
    window_buf,
    adj_send,
    adj_recv,
    adj_rows,
    route_buf,
    focus_sem,
    v_sem,
    u_sem,
    coef_send_sem,
    coef_recv_sem,
    adj_send_sem,
    adj_recv_sem,
    far_send_sem,
    far_recv_sem,
):
    my_col = lax.axis_index("col")
    my_freq = lax.axis_index("freq")
    my_grp = lax.axis_index("grp")
    my_rep = lax.axis_index("rep")
    blocks = focus_buf.shape[0]
    vis = focus_buf.shape[2]
    row_tiles = NR // TS
    col_tiles = NS // TS
    band = blocks * R
    ranks_all = row_tiles * R
    ranks_u = col_tiles * R
    strips = TS // LANES
    quarter = ranks_u // 4
    piece = quarter // CHUNKS
    places = 2 * ROUNDS * count_col
    round_rows = 2 * count_col * R
    peers = [(dx, dz) for dz in (2, 3, 1, 0) for dx in (1, 0) if dx or dz]
    assert len(peers) == 2 * count_col - 1

    def peer_index(dx, dz):
        return dz * 2 + dx - 1

    def place_of(c, freq, col):
        return (c * 2 + freq) * count_col + col

    def focus_copy(b):
        return pltpu.make_async_copy(
            focus_hbm.at[0, :, :, pl.ds(pl.multiple_of(b * TS, TS), TS)], focus_buf.at[b], focus_sem.at[b]
        )

    def v_copy(b):
        return pltpu.make_async_copy(
            v_hbm.at[0, :, :, pl.ds(pl.multiple_of(b * TS, TS), TS)], v_buf.at[b], v_sem.at[b]
        )

    def u_copy(c):
        return pltpu.make_async_copy(u_hbm.at[0, :, 2 * my_freq + c], u_buf.at[c], u_sem.at[c])

    def col_at(dz):
        return lax.rem(my_col + dz, count_col)

    def freq_at(dx):
        return my_freq if dx == 0 else 1 - my_freq

    def device_at(dx, dz):
        return {"freq": freq_at(dx), "col": col_at(dz)}

    def coef_copy(c, dx, dz):
        at = peer_index(dx, dz)
        return pltpu.make_async_remote_copy(
            src_ref=coef_send.at[c, at],
            dst_ref=coef_recv.at[c, my_freq, :, pl.ds(pl.multiple_of(my_col * band, 32), band), :],
            send_sem=coef_send_sem.at[c, at],
            recv_sem=coef_recv_sem.at[c, at],
            device_id=device_at(dx, dz),
            device_id_type=pl.DeviceIdType.MESH,
        )

    def adj_copy(c, dx, dz):
        at = peer_index(dx, dz)
        return pltpu.make_async_remote_copy(
            src_ref=adj_send.at[c, dx, :, pl.ds(pl.multiple_of(col_at(dz) * band, 32), band), :],
            dst_ref=adj_recv.at[place_of(c, my_freq, my_col)],
            send_sem=adj_send_sem.at[c, at],
            recv_sem=adj_recv_sem.at[c, at],
            device_id=device_at(dx, dz),
            device_id_type=pl.DeviceIdType.MESH,
        )

    def far_copy(stage, g):
        c, chunk = divmod(g, CHUNKS)
        grp = 1 - my_grp if stage == 3 else my_grp
        rows = pl.ds(pl.multiple_of((2 * my_rep + grp) * quarter + chunk * piece, 16), piece)
        target = far_u.at[c, :, rows, :]
        source = u_hbm.at[0, :, 2 * (1 - my_freq) + c, rows, :] if stage == 0 else target
        device = ({"freq": 1 - my_freq}, {"grp": 1 - my_grp}, {"rep": 1 - my_rep}, {"rep": 1 - my_rep})[stage]
        return pltpu.make_async_remote_copy(
            src_ref=source,
            dst_ref=target,
            send_sem=far_send_sem.at[stage, g],
            recv_sem=far_recv_sem.at[stage, g],
            device_id=device,
            device_id_type=pl.DeviceIdType.MESH,
        )

    for b in range(blocks):
        focus_copy(b).start()
        v_copy(b).start()
    for c in range(ROUNDS):
        u_copy(c).start()

    barrier = pltpu.get_barrier_semaphore()
    for device in [device_at(dx, dz) for dx, dz in peers] + [{"grp": 1 - my_grp}, {"rep": 1 - my_rep}]:
        pl.semaphore_signal(barrier, inc=1, device_id=device, device_id_type=pl.DeviceIdType.MESH)

    dest_of = []
    for tile in range(row_tiles):
        slot = jnp.int32(0)
        for other in range(tile):
            slot = slot + (owners_ref[other] == owners_ref[tile]).astype(jnp.int32)
        dest_of.append(place_of(slot % ROUNDS, slot // ROUNDS, owners_ref[tile]))

    def divided(ids):
        return jnp.right_shift(ids * (-(-65536 // R)), 16)

    column_ids = lax.broadcasted_iota(jnp.int32, (1, ranks_all), 1)
    row_ids = lax.broadcasted_iota(jnp.int32, (places * R, ranks_all), 0)
    column_tile = divided(column_ids)
    column_level = column_ids - column_tile * R
    row_place = divided(row_ids)
    row_level = row_ids - row_place * R
    column_dest = jnp.zeros_like(column_ids)
    for tile in range(row_tiles):
        column_dest = jnp.where(column_tile == tile, dest_of[tile], column_dest)
    routed = (row_place == column_dest) & (row_level == column_level)
    for b in range(blocks):
        column_rank = jnp.zeros_like(column_ids)
        for tile in range(row_tiles):
            column_rank = jnp.where(
                column_tile == tile, ranks_ref[tile, my_col * blocks + b], column_rank
            )
        kept = routed & (row_level < column_rank)
        route_buf[b] = jnp.where(kept, 1.0, 0.0).astype(jnp.bfloat16)

    def partial_step(b, carry):
        focus_copy(b).wait()
        v_copy(b).wait()
        focus_low = focus_buf[b].reshape(2 * vis, TS).astype(jnp.bfloat16)
        products = stacked_dot(v_buf[b].reshape(2 * ranks_all, TS), focus_low, ((1,), (1,)))
        real_part = products[:ranks_all, :vis] - products[ranks_all:, vis:]
        imag_part = products[:ranks_all, vis:] + products[ranks_all:, :vis]
        partials = jnp.concatenate([real_part, imag_part], axis=1).astype(jnp.bfloat16)
        placed = stacked_dot(route_buf[b], partials, ((1,), (0,)))
        part_buf[b, 0] = placed[:, :vis]
        part_buf[b, 1] = placed[:, vis:]
        return carry

    def slot_partials(place, part):
        start = pl.multiple_of(place * R, 8)
        pieces = [part_buf[b, part, pl.ds(start, R), :] for b in range(blocks)]
        return jnp.concatenate(pieces, axis=0).astype(jnp.bfloat16)

    def send_coefs(c, wanted):
        for dx, dz in peers:
            if dx in wanted:
                place = place_of(c, freq_at(dx), col_at(dz))
                for part in range(2):
                    coef_send[c, peer_index(dx, dz), part] = slot_partials(place, part)
                coef_copy(c, dx, dz).start()

    def keep_coefs(c):
        for part in range(2):
            coef_recv[c, my_freq, part, pl.ds(pl.multiple_of(my_col * band, 32), band), :] = slot_partials(
                place_of(c, my_freq, my_col), part
            )

    def await_coefs(c, wanted):
        for dx, dz in peers:
            if dx in wanted:
                coef_copy(c, dx, dz).wait_recv()

    def place_factors(b):
        for part in range(2):
            chosen = stacked_dot(route_buf[b], v_buf[b, part], ((1,), (0,)))
            v_place[b, part] = chosen.astype(jnp.bfloat16)

    def field_of(coef, factors):
        real_coef = coef[0]
        imag_coef = coef[1]
        left_side = jnp.concatenate(
            [
                jnp.concatenate([real_coef, imag_coef], axis=1),
                jnp.concatenate([-imag_coef, real_coef], axis=1),
            ],
            axis=0,
        )
        return stacked_dot(left_side, factors.reshape(2 * ranks_u, TS), ((0,), (0,)))

    def own_field(c):
        u_copy(c).wait()
        field_buf[0] = field_of(coef_recv[c, my_freq], u_buf[c])

    def far_field(c):
        field_buf[1] = field_of(coef_recv[c, 1 - my_freq], far_u[c])

    def window(c):
        place = place_of(c, my_freq, my_col)
        onset_row = jnp.ones((strips, LANES), jnp.int32)
        for tile in range(row_tiles):
            held = onsets_ref[tile * strips : (tile + 1) * strips, :]
            onset_row = jnp.where(dest_of[tile] == place, held, onset_row)
        rows = [window_rows(onset_row, freq_at(dx)) for dx in range(2)]
        for chunk in range(strips):
            lanes = pl.ds(chunk * LANES, LANES)
            cut = slice(chunk, chunk + 1)
            values = [[field_buf[dx, part * vis : (part + 1) * vis, lanes] for part in range(2)] for dx in range(2)]
            for dx in range(2):
                ordered = values[dx] + values[1 - dx]
                for part in range(2):
                    row = rows[dx][part]
                    total = row[0][cut] * ordered[0]
                    for q in range(1, 4):
                        total = total + row[q][cut] * ordered[q]
                    window_buf[dx, part * vis : (part + 1) * vis, lanes] = total.astype(jnp.bfloat16)

    def adjoint(c, dx):
        factors = (u_buf, far_u)[dx][c].reshape(2 * ranks_u, TS)
        products = stacked_dot(factors, window_buf[dx], ((1,), (1,)))
        adj_send[c, dx, 0] = (products[:ranks_u, :vis] + products[ranks_u:, vis:]).astype(jnp.bfloat16)
        adj_send[c, dx, 1] = (products[:ranks_u, vis:] - products[ranks_u:, :vis]).astype(jnp.bfloat16)
        for px, pz in peers:
            if px == dx:
                adj_copy(c, px, pz).start()
        if dx == 0:
            place = place_of(c, my_freq, my_col)
            for part in range(2):
                adj_recv[place, part] = adj_send[c, 0, part, pl.ds(pl.multiple_of(my_col * band, 32), band), :]

    def gather_round(c):
        for dx, dz in peers:
            adj_copy(c, dx, dz).wait_recv()
        for place in range(c * 2 * count_col, (c + 1) * 2 * count_col):
            for part in range(2):
                rows = adj_recv[place, part].astype(jnp.float32)
                for b in range(blocks):
                    adj_rows[b, place * R : (place + 1) * R, part * vis : (part + 1) * vis] = rows[
                        b * R : (b + 1) * R
                    ]

    def wave_of(c, b):
        held = slice(c * round_rows, (c + 1) * round_rows)
        rows = adj_rows[b, held, :].astype(jnp.bfloat16)
        real_adj = rows[:, :vis]
        imag_adj = rows[:, vis:]
        left_side = jnp.concatenate(
            [
                jnp.concatenate([real_adj, imag_adj], axis=1),
                jnp.concatenate([imag_adj, -real_adj], axis=1),
            ],
            axis=0,
        )
        factors = v_place[b, :, held, :].reshape(2 * round_rows, TS)
        return stacked_dot(left_side, factors, ((0,), (0,))).reshape(2, vis, TS)

    def early_update(b, carry):
        focus_buf[b] = focus_buf[b] - wave_of(0, b)
        return carry

    def late_update(b, carry):
        out_ref[0, :, :, pl.ds(pl.multiple_of(b * TS, TS), TS)] = focus_buf[b] - wave_of(1, b)
        return carry

    def far_start(c):
        for chunk in range(CHUNKS):
            far_copy(0, c * CHUNKS + chunk).start()

    def from_freq(g):
        far_copy(0, g).wait_recv()
        far_copy(1, g).start()
        far_copy(2, g).start()

    def from_grp(g):
        far_copy(1, g).wait_recv()
        far_copy(3, g).start()

    def await_far(c):
        for g in range(c * CHUNKS, (c + 1) * CHUNKS):
            far_copy(2, g).wait_recv()
            far_copy(3, g).wait_recv()

    partial_step(0, 0)
    pl.semaphore_wait(barrier, len(peers) + 2)
    far_start(0)
    lax.fori_loop(1, blocks, partial_step, 0)
    send_coefs(0, (0, 1))
    far_start(1)
    send_coefs(1, (0,))
    keep_coefs(0)
    keep_coefs(1)
    from_freq(0)
    place_factors(0)
    from_freq(1)
    from_grp(0)
    send_coefs(1, (1,))
    place_factors(1)
    from_freq(2)
    from_grp(1)
    await_coefs(0, (0,))
    own_field(0)
    from_grp(2)
    from_freq(3)
    await_coefs(0, (1,))
    await_far(0)
    far_field(0)
    window(0)
    adjoint(0, 0)
    from_freq(4)
    from_grp(3)
    adjoint(0, 1)
    place_factors(2)
    place_factors(3)
    from_freq(5)
    from_grp(4)
    await_coefs(1, (0,))
    own_field(1)
    from_grp(5)
    await_coefs(1, (1,))
    await_far(1)
    far_field(1)
    window(1)
    adjoint(1, 1)
    adjoint(1, 0)
    gather_round(0)
    lax.fori_loop(0, blocks, early_update, 0)
    gather_round(1)
    lax.fori_loop(0, blocks, late_update, 0)

    for c in range(ROUNDS):
        for dx, dz in peers:
            coef_copy(c, dx, dz).wait_send()
            adj_copy(c, dx, dz).wait_send()
    for stage in range(4):
        for g in range(ROUNDS * CHUNKS):
            far_copy(stage, g).wait_send()


def fused_device(focusing, v_factors, u_factors, tile_ranks, owners, onsets):
    count_col = lax.axis_size("col")
    vis = focusing.shape[2]
    sources_dev = focusing.shape[3]
    blocks = sources_dev // TS
    ranks_all = (NR // TS) * R
    ranks_u = (NS // TS) * R
    band = blocks * R
    low = jnp.bfloat16
    peers = 2 * count_col - 1
    places = 2 * ROUNDS * count_col
    dma = pltpu.SemaphoreType.DMA
    scratch = [
        pltpu.VMEM((blocks, 2, vis, TS), jnp.float32),
        pltpu.VMEM((blocks, 2, ranks_all, TS), low),
        pltpu.VMEM((blocks, 2, places * R, TS), low),
        pltpu.VMEM((ROUNDS, 2, ranks_u, TS), low),
        pltpu.VMEM((ROUNDS, 2, ranks_u, TS), low),
        pltpu.VMEM((blocks, 2, places * R, vis), jnp.float32),
        pltpu.VMEM((ROUNDS, peers, 2, band, vis), low),
        pltpu.VMEM((ROUNDS, 2, 2, ranks_u, vis), low),
        pltpu.VMEM((2, 2 * vis, TS), jnp.float32),
        pltpu.VMEM((2, 2 * vis, TS), low),
        pltpu.VMEM((ROUNDS, 2, 2, ranks_u, vis), low),
        pltpu.VMEM((places, 2, band, vis), low),
        pltpu.VMEM((blocks, places * R, 2 * vis), jnp.float32),
        pltpu.VMEM((blocks, places * R, ranks_all), low),
        dma((blocks,)),
        dma((blocks,)),
        dma((ROUNDS,)),
        dma((ROUNDS, peers)),
        dma((ROUNDS, peers)),
        dma((ROUNDS, peers)),
        dma((ROUNDS, peers)),
        dma((4, ROUNDS * CHUNKS)),
        dma((4, ROUNDS * CHUNKS)),
    ]
    return pl.pallas_call(
        functools.partial(fused_kernel, count_col),
        out_shape=pltpu.VMEM(focusing.shape, jnp.float32),
        in_specs=[
            pl.BlockSpec(memory_space=pltpu.SMEM),
            pl.BlockSpec(memory_space=pltpu.SMEM),
            pl.BlockSpec(memory_space=pltpu.VMEM),
            pl.BlockSpec(memory_space=pl.ANY),
            pl.BlockSpec(memory_space=pl.ANY),
            pl.BlockSpec(memory_space=pl.ANY),
        ],
        out_specs=pl.BlockSpec(memory_space=pltpu.VMEM),
        scratch_shapes=scratch,
        compiler_params=pltpu.CompilerParams(
            collective_id=0, has_side_effects=True, vmem_limit_bytes=56 * 1024 * 1024
        ),
        name="marchenko",
    )(owners, tile_ranks, onsets.reshape(NR // LANES, LANES), focusing, v_factors, u_factors)


def choose(focusing, v_factors, u_factors, tile_ranks, owners, onsets):
    whole_blocks = focusing.shape[3] % TS == 0
    paired = lax.axis_size("freq") == 2 and focusing.shape[0] == 1
    replicas = lax.axis_size("grp") == 2 and lax.axis_size("rep") == 2
    slots = u_factors.shape[2] == 2 * ROUNDS and lax.axis_size("col") == 4
    program = fused_device if whole_blocks and paired and replicas and slots else per_device
    return program(focusing, v_factors, u_factors, tile_ranks, owners, onsets)


def solution(mesh):
    return jax.shard_map(
        choose,
        mesh=mesh,
        in_specs=(
            P("freq", None, ("grp", "rep"), "col"),
            P("freq", None, None, "col"),
            P("freq", None, "col", None, None),
            P(),
            P(),
            P(),
        ),
        out_specs=P("freq", None, ("grp", "rep"), "col"),
        check_vma=False,
    )
```

```python
import functools
import math

import jax
import jax.numpy as jnp
from jax import lax
from jax.experimental import pallas as pl
from jax.experimental.pallas import tpu as pltpu
from jax.sharding import PartitionSpec as P

TS = 1024
R = 24
NR = 16384
NS = 16384
NT = 512
KLO = 8
LANES = 128
ROUNDS = 2
CHUNKS = 3


def window_tables(count_freq, onset_rows):
    time_steps = jnp.arange(NT, dtype=jnp.int32)
    freq_bins = KLO + jnp.arange(count_freq, dtype=jnp.int32)
    phases = 2.0 * jnp.pi * (freq_bins[None, :] * time_steps[:, None] % NT).astype(jnp.float32) / NT
    cosine = jnp.cos(phases)
    sines = jnp.sin(phases)
    analyse = jnp.stack([cosine, -sines], axis=2).reshape(NT, 2 * count_freq)
    synthesis = analyse * (2.0 / NT)
    product_table = (analyse[:, :, None] * synthesis[:, None, :]).reshape(
        NT, 4 * count_freq * count_freq
    )
    lower = (time_steps[:, None] >= time_steps[None, :]).astype(jnp.float32)
    running_table = jnp.dot(lower, product_table, precision=lax.Precision.HIGHEST)
    mixing = jnp.take(running_table, onset_rows - 1, axis=0)
    return mixing.reshape(-1, 2 * count_freq, 2 * count_freq)


def kernel_product(einsum_recipe, left_side, right_side):
    return jnp.einsum(einsum_recipe, left_side, right_side, preferred_element_type=jnp.float32)


def per_device(focusing, v_factors, u_factors, tile_ranks, owners, onsets):
    count_col = lax.axis_size("col")
    my_column = lax.axis_index("col")
    count_freq = lax.axis_size("freq")
    my_freq = lax.axis_index("freq")
    freq_dev = focusing.shape[0]
    vis_dev = focusing.shape[2]
    sources_dev = focusing.shape[3]
    capacity = u_factors.shape[2]
    block_width = min(sources_dev, TS)
    blocks_dev = sources_dev // block_width
    per_tile = TS // block_width
    all_blocks = count_col * blocks_dev
    row_tiles = NR // TS
    col_tiles = NS // TS
    freq_all = freq_dev * count_freq
    quarter = TS // count_freq
    tile_ids = jnp.arange(row_tiles, dtype=jnp.int32)
    same_owner = owners[:, None] == owners[None, :]
    earlier = tile_ids[None, :] < tile_ids[:, None]
    slot_of = jnp.sum((same_owner & earlier).astype(jnp.int32), axis=1)
    slot_ids = jnp.arange(capacity, dtype=jnp.int32)
    routing = (owners[None, None, :] == jnp.arange(count_col, dtype=jnp.int32)[:, None, None]) & (
        slot_of[None, None, :] == slot_ids[None, :, None]
    )
    lower_routing = routing.astype(jnp.bfloat16)
    my_slots = ((owners[None, :] == my_column) & (slot_of[None, :] == slot_ids[:, None])).astype(
        jnp.int32
    )
    slot_ranks = jnp.sum(my_slots[:, :, None] * tile_ranks[None, :, :], axis=1)
    rank_mask = (jnp.arange(R, dtype=jnp.int32)[None, None, :] < slot_ranks[:, :, None]).astype(
        jnp.float32
    )
    slot_onsets = jnp.sum(my_slots[:, :, None] * onsets.reshape(row_tiles, TS)[None], axis=1)
    slot_onsets = jnp.maximum(slot_onsets, 1)
    focus_low = focusing.astype(jnp.bfloat16).reshape(freq_dev, 2, vis_dev, blocks_dev, block_width)
    factors_v = v_factors.reshape(freq_dev, 2, row_tiles, R, blocks_dev, block_width)
    einsum_recipe = "fikbs,fvbs->ifbkv"
    real_portion = kernel_product(einsum_recipe, factors_v[:, 0], focus_low[:, 0]) - kernel_product(
        einsum_recipe, factors_v[:, 1], focus_low[:, 1]
    )
    part_imag = kernel_product(einsum_recipe, factors_v[:, 0], focus_low[:, 1]) + kernel_product(
        einsum_recipe, factors_v[:, 1], focus_low[:, 0]
    )
    partial_sums = jnp.stack([real_portion, part_imag], axis=3).astype(jnp.bfloat16)
    outgoing_parts = kernel_product("way,ymleno->amwleno", lower_routing, partial_sums).astype(
        jnp.bfloat16
    )
    outgoing_parts = outgoing_parts.reshape(capacity, freq_dev, all_blocks, 2, R, vis_dev)
    arrived = lax.all_to_all(outgoing_parts, "col", split_axis=2, concat_axis=2, tiled=True)
    coefficients = jnp.sum(
        arrived.astype(jnp.float32).reshape(capacity, freq_dev, col_tiles, per_tile, 2, R, vis_dev),
        axis=3,
    )
    coefficients = (coefficients * rank_mask[:, None, :, None, :, None]).astype(jnp.bfloat16)
    factors_u = u_factors.reshape(freq_dev, 2, capacity, col_tiles, R, TS)
    uform = "fcjka,cfjkv->cfav"
    field_real = kernel_product(uform, factors_u[:, 0], coefficients[:, :, :, 0]) - kernel_product(
        uform, factors_u[:, 1], coefficients[:, :, :, 1]
    )
    field_imag = kernel_product(uform, factors_u[:, 0], coefficients[:, :, :, 1]) + kernel_product(
        uform, factors_u[:, 1], coefficients[:, :, :, 0]
    )
    receiver_field = jnp.stack([field_real, field_imag], axis=2).astype(jnp.bfloat16)
    turned = lax.all_to_all(receiver_field, "freq", split_axis=3, concat_axis=1, tiled=True)
    quarter_onsets = lax.dynamic_slice_in_dim(slot_onsets, my_freq * quarter, quarter, 1)
    mixing = window_tables(freq_all, quarter_onsets.reshape(-1)).reshape(
        capacity, quarter, 2 * freq_all, 2 * freq_all
    )
    flat_field = turned.reshape(capacity, 2 * freq_all, quarter, vis_dev).astype(jnp.float32)
    mixed_field = jnp.einsum("crpq,cqrv->cprv", mixing, flat_field, precision=lax.Precision.HIGHEST)
    mixed_field = mixed_field.astype(jnp.bfloat16).reshape(capacity, freq_all, 2, quarter, vis_dev)
    windowed = lax.all_to_all(mixed_field, "freq", split_axis=1, concat_axis=3, tiled=True)
    aform = "fcjka,cfav->cfjkv"
    back_real = kernel_product(aform, factors_u[:, 0], windowed[:, :, 0]) + kernel_product(
        aform, factors_u[:, 1], windowed[:, :, 1]
    )
    back_imag = kernel_product(aform, factors_u[:, 0], windowed[:, :, 1]) - kernel_product(
        aform, factors_u[:, 1], windowed[:, :, 0]
    )
    adjoint = jnp.stack([back_real, back_imag], axis=3) * rank_mask[:, None, :, None, :, None]
    adjoint = adjoint.astype(jnp.bfloat16)
    spread = jnp.broadcast_to(
        adjoint[:, :, :, None], (capacity, freq_dev, col_tiles, per_tile, 2, R, vis_dev)
    )
    spread = spread.reshape(capacity, freq_dev, all_blocks, 2, R, vis_dev)
    result_field = lax.all_to_all(spread, "col", split_axis=2, concat_axis=2, tiled=True)
    result_field = result_field.reshape(capacity, freq_dev, count_col, blocks_dev, 2, R, vis_dev)
    row_share = kernel_product("prq,rjpagwu->qjagwu", lower_routing, result_field).astype(
        jnp.bfloat16
    )
    wform = "fikbs,ifbkv->fvbs"
    wave_real = kernel_product(wform, factors_v[:, 0], row_share[:, :, :, 0]) + kernel_product(
        wform, factors_v[:, 1], row_share[:, :, :, 1]
    )
    wave_imag = kernel_product(wform, factors_v[:, 0], row_share[:, :, :, 1]) - kernel_product(
        wform, factors_v[:, 1], row_share[:, :, :, 0]
    )
    wave_field = jnp.stack([wave_real, wave_imag], axis=1).reshape(
        freq_dev, 2, vis_dev, sources_dev
    )
    return focusing - wave_field


def window_rows(onset_row, my_freq):
    sign = (2 * my_freq - 1).astype(jnp.float32)

    def sums(bins, inverse):
        phase_all = jnp.bitwise_and(bins * onset_row, 2 * NT - 1).astype(jnp.float32) * (math.pi / NT)
        phase_less = jnp.bitwise_and(bins * (onset_row - 1), 2 * NT - 1).astype(jnp.float32) * (math.pi / NT)
        scaled = jnp.sin(phase_all) * inverse
        return jnp.cos(phase_less) * scaled, jnp.sin(phase_less) * scaled

    def inverse_of(bins):
        return 1.0 / (NT * math.sin(math.pi * bins / NT))

    own_inverse = jnp.where(my_freq == 0, inverse_of(2 * KLO), inverse_of(2 * KLO + 2))
    own_cos, own_sin = sums(2 * KLO + 2 * my_freq, own_inverse)
    sum_cos, sum_sin = sums(2 * KLO + 1, inverse_of(2 * KLO + 1))
    gap_cos, gap_sin = sums(1, inverse_of(1))
    level = onset_row.astype(jnp.float32) * (1.0 / NT)
    real_row = (level + own_cos, -own_sin, gap_cos + sum_cos, sign * gap_sin - sum_sin)
    imag_row = (-own_sin, level - own_cos, -sum_sin - sign * gap_sin, gap_cos - sum_cos)
    return real_row, imag_row


def stacked_dot(left_side, right_side, dims):
    return lax.dot_general(left_side, right_side, (dims, ((), ())), preferred_element_type=jnp.float32)


def fused_kernel(
    count_col,
    owners_ref,
    ranks_ref,
    onsets_ref,
    focus_hbm,
    v_hbm,
    u_hbm,
    out_ref,
    focus_buf,
    v_buf,
    v_place,
    u_buf,
    far_u,
    part_buf,
    coef_send,
    coef_recv,
    field_buf,
    window_buf,
    adj_send,
    adj_recv,
    adj_rows,
    route_buf,
    focus_sem,
    v_sem,
    u_sem,
    coef_send_sem,
    coef_recv_sem,
    adj_send_sem,
    adj_recv_sem,
    far_send_sem,
    far_recv_sem,
):
    my_col = lax.axis_index("col")
    my_freq = lax.axis_index("freq")
    my_grp = lax.axis_index("grp")
    my_rep = lax.axis_index("rep")
    blocks = focus_buf.shape[0]
    vis = focus_buf.shape[2]
    row_tiles = NR // TS
    col_tiles = NS // TS
    band = blocks * R
    ranks_all = row_tiles * R
    ranks_u = col_tiles * R
    strips = TS // LANES
    quarter = ranks_u // 4
    piece = quarter // CHUNKS
    places = 2 * ROUNDS * count_col
    round_rows = 2 * count_col * R
    peers = [(dx, dz) for dz in (2, 3, 1, 0) for dx in (1, 0) if dx or dz]
    assert len(peers) == 2 * count_col - 1

    def peer_index(dx, dz):
        return dz * 2 + dx - 1

    def place_of(c, freq, col):
        return (c * 2 + freq) * count_col + col

    def focus_copy(b):
        return pltpu.make_async_copy(
            focus_hbm.at[0, :, :, pl.ds(pl.multiple_of(b * TS, TS), TS)], focus_buf.at[b], focus_sem.at[b]
        )

    def v_copy(b):
        return pltpu.make_async_copy(
            v_hbm.at[0, :, :, pl.ds(pl.multiple_of(b * TS, TS), TS)], v_buf.at[b], v_sem.at[b]
        )

    def u_copy(c):
        return pltpu.make_async_copy(u_hbm.at[0, :, 2 * my_freq + c], u_buf.at[c], u_sem.at[c])

    def col_at(dz):
        return lax.rem(my_col + dz, count_col)

    def freq_at(dx):
        return my_freq if dx == 0 else 1 - my_freq

    def device_at(dx, dz):
        return {"freq": freq_at(dx), "col": col_at(dz)}

    def coef_copy(c, dx, dz):
        at = peer_index(dx, dz)
        return pltpu.make_async_remote_copy(
            src_ref=coef_send.at[c, at],
            dst_ref=coef_recv.at[c, my_freq, :, pl.ds(pl.multiple_of(my_col * band, 32), band), :],
            send_sem=coef_send_sem.at[c, at],
            recv_sem=coef_recv_sem.at[c, at],
            device_id=device_at(dx, dz),
            device_id_type=pl.DeviceIdType.MESH,
        )

    def adj_copy(c, dx, dz):
        at = peer_index(dx, dz)
        return pltpu.make_async_remote_copy(
            src_ref=adj_send.at[c, dx, :, pl.ds(pl.multiple_of(col_at(dz) * band, 32), band), :],
            dst_ref=adj_recv.at[place_of(c, my_freq, my_col)],
            send_sem=adj_send_sem.at[c, at],
            recv_sem=adj_recv_sem.at[c, at],
            device_id=device_at(dx, dz),
            device_id_type=pl.DeviceIdType.MESH,
        )

    def far_copy(stage, g):
        c, chunk = divmod(g, CHUNKS)
        grp = 1 - my_grp if stage == 3 else my_grp
        rows = pl.ds(pl.multiple_of((2 * my_rep + grp) * quarter + chunk * piece, 16), piece)
        target = far_u.at[c, :, rows, :]
        source = u_hbm.at[0, :, 2 * (1 - my_freq) + c, rows, :] if stage == 0 else target
        device = ({"freq": 1 - my_freq}, {"grp": 1 - my_grp}, {"rep": 1 - my_rep}, {"rep": 1 - my_rep})[stage]
        return pltpu.make_async_remote_copy(
            src_ref=source,
            dst_ref=target,
            send_sem=far_send_sem.at[stage, g],
            recv_sem=far_recv_sem.at[stage, g],
            device_id=device,
            device_id_type=pl.DeviceIdType.MESH,
        )

    def far_start(c):
        for chunk in range(CHUNKS):
            far_copy(0, c * CHUNKS + chunk).start()

    barrier = pltpu.get_barrier_semaphore()
    for device in [device_at(dx, dz) for dx, dz in peers] + [{"grp": 1 - my_grp}, {"rep": 1 - my_rep}]:
        pl.semaphore_signal(barrier, inc=1, device_id=device, device_id_type=pl.DeviceIdType.MESH)

    for b in range(blocks):
        focus_copy(b).start()
        v_copy(b).start()
    for c in range(ROUNDS):
        u_copy(c).start()

    pl.semaphore_wait(barrier, len(peers) + 2)
    far_start(0)

    dest_of = []
    for tile in range(row_tiles):
        slot = jnp.int32(0)
        for other in range(tile):
            slot = slot + (owners_ref[other] == owners_ref[tile]).astype(jnp.int32)
        dest_of.append(place_of(slot % ROUNDS, slot // ROUNDS, owners_ref[tile]))

    def divided(ids):
        return jnp.right_shift(ids * (-(-65536 // R)), 16)

    column_ids = lax.broadcasted_iota(jnp.int32, (1, ranks_all), 1)
    row_ids = lax.broadcasted_iota(jnp.int32, (places * R, ranks_all), 0)
    column_tile = divided(column_ids)
    column_level = column_ids - column_tile * R
    row_place = divided(row_ids)
    row_level = row_ids - row_place * R
    column_dest = jnp.zeros_like(column_ids)
    for tile in range(row_tiles):
        column_dest = jnp.where(column_tile == tile, dest_of[tile], column_dest)
    routed = (row_place == column_dest) & (row_level == column_level)
    for b in range(blocks):
        column_rank = jnp.zeros_like(column_ids)
        for tile in range(row_tiles):
            column_rank = jnp.where(
                column_tile == tile, ranks_ref[tile, my_col * blocks + b], column_rank
            )
        kept = routed & (row_level < column_rank)
        route_buf[b] = jnp.where(kept, 1.0, 0.0).astype(jnp.bfloat16)

    def partial_step(b, carry):
        focus_copy(b).wait()
        v_copy(b).wait()
        focus_low = focus_buf[b].reshape(2 * vis, TS).astype(jnp.bfloat16)
        products = stacked_dot(v_buf[b].reshape(2 * ranks_all, TS), focus_low, ((1,), (1,)))
        real_part = products[:ranks_all, :vis] - products[ranks_all:, vis:]
        imag_part = products[:ranks_all, vis:] + products[ranks_all:, :vis]
        partials = jnp.concatenate([real_part, imag_part], axis=1).astype(jnp.bfloat16)
        placed = stacked_dot(route_buf[b], partials, ((1,), (0,)))
        part_buf[b, 0] = placed[:, :vis]
        part_buf[b, 1] = placed[:, vis:]
        return carry

    def slot_partials(place, part):
        start = pl.multiple_of(place * R, 8)
        pieces = [part_buf[b, part, pl.ds(start, R), :] for b in range(blocks)]
        return jnp.concatenate(pieces, axis=0).astype(jnp.bfloat16)

    def send_coefs(c, wanted):
        for dx, dz in peers:
            if dx in wanted:
                place = place_of(c, freq_at(dx), col_at(dz))
                for part in range(2):
                    coef_send[c, peer_index(dx, dz), part] = slot_partials(place, part)
                coef_copy(c, dx, dz).start()

    def keep_coefs(c):
        for part in range(2):
            coef_recv[c, my_freq, part, pl.ds(pl.multiple_of(my_col * band, 32), band), :] = slot_partials(
                place_of(c, my_freq, my_col), part
            )

    def await_coefs(c, wanted):
        for dx, dz in peers:
            if dx in wanted:
                coef_copy(c, dx, dz).wait_recv()

    def place_factors(b):
        for part in range(2):
            chosen = stacked_dot(route_buf[b], v_buf[b, part], ((1,), (0,)))
            v_place[b, part] = chosen.astype(jnp.bfloat16)

    def field_of(coef, factors):
        real_coef = coef[0]
        imag_coef = coef[1]
        left_side = jnp.concatenate(
            [
                jnp.concatenate([real_coef, imag_coef], axis=1),
                jnp.concatenate([-imag_coef, real_coef], axis=1),
            ],
            axis=0,
        )
        return stacked_dot(left_side, factors.reshape(2 * ranks_u, TS), ((0,), (0,)))

    def own_field(c):
        u_copy(c).wait()
        field_buf[0] = field_of(coef_recv[c, my_freq], u_buf[c])

    def far_field(c):
        field_buf[1] = field_of(coef_recv[c, 1 - my_freq], far_u[c])

    def window(c):
        place = place_of(c, my_freq, my_col)
        onset_row = jnp.ones((strips, LANES), jnp.int32)
        for tile in range(row_tiles):
            held = onsets_ref[tile * strips : (tile + 1) * strips, :]
            onset_row = jnp.where(dest_of[tile] == place, held, onset_row)
        rows = [window_rows(onset_row, freq_at(dx)) for dx in range(2)]
        for chunk in range(strips):
            lanes = pl.ds(chunk * LANES, LANES)
            cut = slice(chunk, chunk + 1)
            values = [[field_buf[dx, part * vis : (part + 1) * vis, lanes] for part in range(2)] for dx in range(2)]
            for dx in range(2):
                ordered = values[dx] + values[1 - dx]
                for part in range(2):
                    row = rows[dx][part]
                    total = row[0][cut] * ordered[0]
                    for q in range(1, 4):
                        total = total + row[q][cut] * ordered[q]
                    window_buf[dx, part * vis : (part + 1) * vis, lanes] = total.astype(jnp.bfloat16)

    def adjoint(c, dx):
        factors = (u_buf, far_u)[dx][c].reshape(2 * ranks_u, TS)
        products = stacked_dot(factors, window_buf[dx], ((1,), (1,)))
        adj_send[c, dx, 0] = (products[:ranks_u, :vis] + products[ranks_u:, vis:]).astype(jnp.bfloat16)
        adj_send[c, dx, 1] = (products[:ranks_u, vis:] - products[ranks_u:, :vis]).astype(jnp.bfloat16)
        if dx == 0:
            place = place_of(c, my_freq, my_col)
            for part in range(2):
                adj_recv[place, part] = adj_send[c, 0, part, pl.ds(pl.multiple_of(my_col * band, 32), band), :]

    def send_adjoint(c, dx):
        for px, pz in peers:
            if px == dx:
                adj_copy(c, px, pz).start()

    def gather_round(c):
        for dx, dz in peers:
            adj_copy(c, dx, dz).wait_recv()
        for place in range(c * 2 * count_col, (c + 1) * 2 * count_col):
            for part in range(2):
                rows = adj_recv[place, part].astype(jnp.float32)
                for b in range(blocks):
                    adj_rows[b, place * R : (place + 1) * R, part * vis : (part + 1) * vis] = rows[
                        b * R : (b + 1) * R
                    ]

    def wave_of(c, b):
        held = slice(c * round_rows, (c + 1) * round_rows)
        rows = adj_rows[b, held, :].astype(jnp.bfloat16)
        real_adj = rows[:, :vis]
        imag_adj = rows[:, vis:]
        left_side = jnp.concatenate(
            [
                jnp.concatenate([real_adj, imag_adj], axis=1),
                jnp.concatenate([imag_adj, -real_adj], axis=1),
            ],
            axis=0,
        )
        factors = v_place[b, :, held, :].reshape(2 * round_rows, TS)
        return stacked_dot(left_side, factors, ((0,), (0,))).reshape(2, vis, TS)

    def early_update(b, carry):
        focus_buf[b] = focus_buf[b] - wave_of(0, b)
        return carry

    def late_update(b, carry):
        out_ref[0, :, :, pl.ds(pl.multiple_of(b * TS, TS), TS)] = focus_buf[b] - wave_of(1, b)
        return carry

    def from_freq(g):
        far_copy(0, g).wait_recv()
        far_copy(1, g).start()
        far_copy(2, g).start()

    def from_grp(g):
        far_copy(1, g).wait_recv()
        far_copy(3, g).start()

    def await_far(c):
        for g in range(c * CHUNKS, (c + 1) * CHUNKS):
            far_copy(2, g).wait_recv()
            far_copy(3, g).wait_recv()

    partial_step(0, 0)
    lax.fori_loop(1, blocks, partial_step, 0)
    send_coefs(0, (1,))
    send_coefs(0, (0,))
    far_start(1)
    send_coefs(1, (0,))
    keep_coefs(0)
    keep_coefs(1)
    from_freq(0)
    place_factors(0)
    from_freq(1)
    from_grp(0)
    place_factors(1)
    from_freq(2)
    from_grp(1)
    await_coefs(0, (0,))
    own_field(0)
    from_grp(2)
    from_freq(3)
    send_coefs(1, (1,))
    await_coefs(0, (1,))
    await_far(0)
    far_field(0)
    window(0)
    adjoint(0, 0)
    send_adjoint(0, 0)
    from_freq(4)
    from_grp(3)
    adjoint(0, 1)
    place_factors(2)
    place_factors(3)
    from_freq(5)
    from_grp(4)
    send_adjoint(0, 1)
    await_coefs(1, (0,))
    own_field(1)
    from_grp(5)
    await_coefs(1, (1,))
    await_far(1)
    far_field(1)
    window(1)
    adjoint(1, 1)
    send_adjoint(1, 1)
    adjoint(1, 0)
    send_adjoint(1, 0)
    gather_round(0)
    lax.fori_loop(0, blocks, early_update, 0)
    gather_round(1)
    lax.fori_loop(0, blocks, late_update, 0)

    for c in range(ROUNDS):
        for dx, dz in peers:
            coef_copy(c, dx, dz).wait_send()
            adj_copy(c, dx, dz).wait_send()
    for stage in range(4):
        for g in range(ROUNDS * CHUNKS):
            far_copy(stage, g).wait_send()


def fused_device(focusing, v_factors, u_factors, tile_ranks, owners, onsets):
    count_col = lax.axis_size("col")
    vis = focusing.shape[2]
    sources_dev = focusing.shape[3]
    blocks = sources_dev // TS
    ranks_all = (NR // TS) * R
    ranks_u = (NS // TS) * R
    band = blocks * R
    low = jnp.bfloat16
    peers = 2 * count_col - 1
    places = 2 * ROUNDS * count_col
    dma = pltpu.SemaphoreType.DMA
    scratch = [
        pltpu.VMEM((blocks, 2, vis, TS), jnp.float32),
        pltpu.VMEM((blocks, 2, ranks_all, TS), low),
        pltpu.VMEM((blocks, 2, places * R, TS), low),
        pltpu.VMEM((ROUNDS, 2, ranks_u, TS), low),
        pltpu.VMEM((ROUNDS, 2, ranks_u, TS), low),
        pltpu.VMEM((blocks, 2, places * R, vis), jnp.float32),
        pltpu.VMEM((ROUNDS, peers, 2, band, vis), low),
        pltpu.VMEM((ROUNDS, 2, 2, ranks_u, vis), low),
        pltpu.VMEM((2, 2 * vis, TS), jnp.float32),
        pltpu.VMEM((2, 2 * vis, TS), low),
        pltpu.VMEM((ROUNDS, 2, 2, ranks_u, vis), low),
        pltpu.VMEM((places, 2, band, vis), low),
        pltpu.VMEM((blocks, places * R, 2 * vis), jnp.float32),
        pltpu.VMEM((blocks, places * R, ranks_all), low),
        dma((blocks,)),
        dma((blocks,)),
        dma((ROUNDS,)),
        dma((ROUNDS, peers)),
        dma((ROUNDS, peers)),
        dma((ROUNDS, peers)),
        dma((ROUNDS, peers)),
        dma((4, ROUNDS * CHUNKS)),
        dma((4, ROUNDS * CHUNKS)),
    ]
    return pl.pallas_call(
        functools.partial(fused_kernel, count_col),
        out_shape=pltpu.VMEM(focusing.shape, jnp.float32),
        in_specs=[
            pl.BlockSpec(memory_space=pltpu.SMEM),
            pl.BlockSpec(memory_space=pltpu.SMEM),
            pl.BlockSpec(memory_space=pltpu.VMEM),
            pl.BlockSpec(memory_space=pl.ANY),
            pl.BlockSpec(memory_space=pl.ANY),
            pl.BlockSpec(memory_space=pl.ANY),
        ],
        out_specs=pl.BlockSpec(memory_space=pltpu.VMEM),
        scratch_shapes=scratch,
        compiler_params=pltpu.CompilerParams(
            collective_id=0, has_side_effects=True, vmem_limit_bytes=56 * 1024 * 1024
        ),
        name="marchenko",
    )(owners, tile_ranks, onsets.reshape(NR // LANES, LANES), focusing, v_factors, u_factors)


def choose(focusing, v_factors, u_factors, tile_ranks, owners, onsets):
    whole_blocks = focusing.shape[3] % TS == 0
    paired = lax.axis_size("freq") == 2 and focusing.shape[0] == 1
    replicas = lax.axis_size("grp") == 2 and lax.axis_size("rep") == 2
    slots = u_factors.shape[2] == 2 * ROUNDS and lax.axis_size("col") == 4
    program = fused_device if whole_blocks and paired and replicas and slots else per_device
    return program(focusing, v_factors, u_factors, tile_ranks, owners, onsets)


def solution(mesh):
    return jax.shard_map(
        choose,
        mesh=mesh,
        in_specs=(
            P("freq", None, ("grp", "rep"), "col"),
            P("freq", None, None, "col"),
            P("freq", None, "col", None, None),
            P(),
            P(),
            P(),
        ),
        out_specs=P("freq", None, ("grp", "rep"), "col"),
        check_vma=False,
    )
```

```python
import functools
import math

import jax
import jax.numpy as jnp
from jax import lax
from jax.experimental import pallas as pl
from jax.experimental.pallas import tpu as pltpu
from jax.sharding import PartitionSpec as P

TS = 1024
R = 24
NR = 16384
NS = 16384
NT = 512
KLO = 8
LANES = 128
ROUNDS = 2
CHUNKS = 3
FIRST_VMEM = 50


def window_tables(count_freq, onset_rows):
    time_steps = jnp.arange(NT, dtype=jnp.int32)
    freq_bins = KLO + jnp.arange(count_freq, dtype=jnp.int32)
    phases = 2.0 * jnp.pi * (freq_bins[None, :] * time_steps[:, None] % NT).astype(jnp.float32) / NT
    cosine = jnp.cos(phases)
    sines = jnp.sin(phases)
    analyse = jnp.stack([cosine, -sines], axis=2).reshape(NT, 2 * count_freq)
    synthesis = analyse * (2.0 / NT)
    product_table = (analyse[:, :, None] * synthesis[:, None, :]).reshape(
        NT, 4 * count_freq * count_freq
    )
    lower = (time_steps[:, None] >= time_steps[None, :]).astype(jnp.float32)
    running_table = jnp.dot(lower, product_table, precision=lax.Precision.HIGHEST)
    mixing = jnp.take(running_table, onset_rows - 1, axis=0)
    return mixing.reshape(-1, 2 * count_freq, 2 * count_freq)


def kernel_product(einsum_recipe, left_side, right_side):
    return jnp.einsum(einsum_recipe, left_side, right_side, preferred_element_type=jnp.float32)


def per_device(focusing, v_factors, u_factors, tile_ranks, owners, onsets):
    count_col = lax.axis_size("col")
    my_column = lax.axis_index("col")
    count_freq = lax.axis_size("freq")
    my_freq = lax.axis_index("freq")
    freq_dev = focusing.shape[0]
    vis_dev = focusing.shape[2]
    sources_dev = focusing.shape[3]
    capacity = u_factors.shape[2]
    block_width = min(sources_dev, TS)
    blocks_dev = sources_dev // block_width
    per_tile = TS // block_width
    all_blocks = count_col * blocks_dev
    row_tiles = NR // TS
    col_tiles = NS // TS
    freq_all = freq_dev * count_freq
    quarter = TS // count_freq
    tile_ids = jnp.arange(row_tiles, dtype=jnp.int32)
    same_owner = owners[:, None] == owners[None, :]
    earlier = tile_ids[None, :] < tile_ids[:, None]
    slot_of = jnp.sum((same_owner & earlier).astype(jnp.int32), axis=1)
    slot_ids = jnp.arange(capacity, dtype=jnp.int32)
    routing = (owners[None, None, :] == jnp.arange(count_col, dtype=jnp.int32)[:, None, None]) & (
        slot_of[None, None, :] == slot_ids[None, :, None]
    )
    lower_routing = routing.astype(jnp.bfloat16)
    my_slots = ((owners[None, :] == my_column) & (slot_of[None, :] == slot_ids[:, None])).astype(
        jnp.int32
    )
    slot_ranks = jnp.sum(my_slots[:, :, None] * tile_ranks[None, :, :], axis=1)
    rank_mask = (jnp.arange(R, dtype=jnp.int32)[None, None, :] < slot_ranks[:, :, None]).astype(
        jnp.float32
    )
    slot_onsets = jnp.sum(my_slots[:, :, None] * onsets.reshape(row_tiles, TS)[None], axis=1)
    slot_onsets = jnp.maximum(slot_onsets, 1)
    focus_low = focusing.astype(jnp.bfloat16).reshape(freq_dev, 2, vis_dev, blocks_dev, block_width)
    factors_v = v_factors.reshape(freq_dev, 2, row_tiles, R, blocks_dev, block_width)
    einsum_recipe = "fikbs,fvbs->ifbkv"
    real_portion = kernel_product(einsum_recipe, factors_v[:, 0], focus_low[:, 0]) - kernel_product(
        einsum_recipe, factors_v[:, 1], focus_low[:, 1]
    )
    part_imag = kernel_product(einsum_recipe, factors_v[:, 0], focus_low[:, 1]) + kernel_product(
        einsum_recipe, factors_v[:, 1], focus_low[:, 0]
    )
    partial_sums = jnp.stack([real_portion, part_imag], axis=3).astype(jnp.bfloat16)
    outgoing_parts = kernel_product("way,ymleno->amwleno", lower_routing, partial_sums).astype(
        jnp.bfloat16
    )
    outgoing_parts = outgoing_parts.reshape(capacity, freq_dev, all_blocks, 2, R, vis_dev)
    arrived = lax.all_to_all(outgoing_parts, "col", split_axis=2, concat_axis=2, tiled=True)
    coefficients = jnp.sum(
        arrived.astype(jnp.float32).reshape(capacity, freq_dev, col_tiles, per_tile, 2, R, vis_dev),
        axis=3,
    )
    coefficients = (coefficients * rank_mask[:, None, :, None, :, None]).astype(jnp.bfloat16)
    factors_u = u_factors.reshape(freq_dev, 2, capacity, col_tiles, R, TS)
    uform = "fcjka,cfjkv->cfav"
    field_real = kernel_product(uform, factors_u[:, 0], coefficients[:, :, :, 0]) - kernel_product(
        uform, factors_u[:, 1], coefficients[:, :, :, 1]
    )
    field_imag = kernel_product(uform, factors_u[:, 0], coefficients[:, :, :, 1]) + kernel_product(
        uform, factors_u[:, 1], coefficients[:, :, :, 0]
    )
    receiver_field = jnp.stack([field_real, field_imag], axis=2).astype(jnp.bfloat16)
    turned = lax.all_to_all(receiver_field, "freq", split_axis=3, concat_axis=1, tiled=True)
    quarter_onsets = lax.dynamic_slice_in_dim(slot_onsets, my_freq * quarter, quarter, 1)
    mixing = window_tables(freq_all, quarter_onsets.reshape(-1)).reshape(
        capacity, quarter, 2 * freq_all, 2 * freq_all
    )
    flat_field = turned.reshape(capacity, 2 * freq_all, quarter, vis_dev).astype(jnp.float32)
    mixed_field = jnp.einsum("crpq,cqrv->cprv", mixing, flat_field, precision=lax.Precision.HIGHEST)
    mixed_field = mixed_field.astype(jnp.bfloat16).reshape(capacity, freq_all, 2, quarter, vis_dev)
    windowed = lax.all_to_all(mixed_field, "freq", split_axis=1, concat_axis=3, tiled=True)
    aform = "fcjka,cfav->cfjkv"
    back_real = kernel_product(aform, factors_u[:, 0], windowed[:, :, 0]) + kernel_product(
        aform, factors_u[:, 1], windowed[:, :, 1]
    )
    back_imag = kernel_product(aform, factors_u[:, 0], windowed[:, :, 1]) - kernel_product(
        aform, factors_u[:, 1], windowed[:, :, 0]
    )
    adjoint = jnp.stack([back_real, back_imag], axis=3) * rank_mask[:, None, :, None, :, None]
    adjoint = adjoint.astype(jnp.bfloat16)
    spread = jnp.broadcast_to(
        adjoint[:, :, :, None], (capacity, freq_dev, col_tiles, per_tile, 2, R, vis_dev)
    )
    spread = spread.reshape(capacity, freq_dev, all_blocks, 2, R, vis_dev)
    result_field = lax.all_to_all(spread, "col", split_axis=2, concat_axis=2, tiled=True)
    result_field = result_field.reshape(capacity, freq_dev, count_col, blocks_dev, 2, R, vis_dev)
    row_share = kernel_product("prq,rjpagwu->qjagwu", lower_routing, result_field).astype(
        jnp.bfloat16
    )
    wform = "fikbs,ifbkv->fvbs"
    wave_real = kernel_product(wform, factors_v[:, 0], row_share[:, :, :, 0]) + kernel_product(
        wform, factors_v[:, 1], row_share[:, :, :, 1]
    )
    wave_imag = kernel_product(wform, factors_v[:, 0], row_share[:, :, :, 1]) - kernel_product(
        wform, factors_v[:, 1], row_share[:, :, :, 0]
    )
    wave_field = jnp.stack([wave_real, wave_imag], axis=1).reshape(
        freq_dev, 2, vis_dev, sources_dev
    )
    return focusing - wave_field


def window_rows(onset_row, my_freq):
    sign = (2 * my_freq - 1).astype(jnp.float32)

    def sums(bins, inverse):
        phase_all = jnp.bitwise_and(bins * onset_row, 2 * NT - 1).astype(jnp.float32) * (math.pi / NT)
        phase_less = jnp.bitwise_and(bins * (onset_row - 1), 2 * NT - 1).astype(jnp.float32) * (math.pi / NT)
        scaled = jnp.sin(phase_all) * inverse
        return jnp.cos(phase_less) * scaled, jnp.sin(phase_less) * scaled

    def inverse_of(bins):
        return 1.0 / (NT * math.sin(math.pi * bins / NT))

    own_inverse = jnp.where(my_freq == 0, inverse_of(2 * KLO), inverse_of(2 * KLO + 2))
    own_cos, own_sin = sums(2 * KLO + 2 * my_freq, own_inverse)
    sum_cos, sum_sin = sums(2 * KLO + 1, inverse_of(2 * KLO + 1))
    gap_cos, gap_sin = sums(1, inverse_of(1))
    level = onset_row.astype(jnp.float32) * (1.0 / NT)
    real_row = (level + own_cos, -own_sin, gap_cos + sum_cos, sign * gap_sin - sum_sin)
    imag_row = (-own_sin, level - own_cos, -sum_sin - sign * gap_sin, gap_cos - sum_cos)
    return real_row, imag_row


def stacked_dot(left_side, right_side, dims):
    return lax.dot_general(left_side, right_side, (dims, ((), ())), preferred_element_type=jnp.float32)


def fused_kernel(
    count_col,
    owners_ref,
    ranks_ref,
    onsets_ref,
    focus_hbm,
    v_hbm,
    u_hbm,
    focus_buf,
    v_place,
    last_left,
    v_buf,
    u_buf,
    far_u,
    part_buf,
    coef_send,
    coef_recv,
    field_buf,
    window_buf,
    adj_send,
    adj_recv,
    adj_rows,
    route_buf,
    focus_sem,
    v_sem,
    u_sem,
    coef_send_sem,
    coef_recv_sem,
    adj_send_sem,
    adj_recv_sem,
    far_send_sem,
    far_recv_sem,
):
    my_col = lax.axis_index("col")
    my_freq = lax.axis_index("freq")
    my_grp = lax.axis_index("grp")
    my_rep = lax.axis_index("rep")
    blocks = focus_buf.shape[0]
    vis = focus_buf.shape[2]
    row_tiles = NR // TS
    col_tiles = NS // TS
    band = blocks * R
    ranks_all = row_tiles * R
    ranks_u = col_tiles * R
    strips = TS // LANES
    quarter = ranks_u // 4
    piece = quarter // CHUNKS
    places = 2 * ROUNDS * count_col
    round_rows = 2 * count_col * R
    peers = [(dx, dz) for dz in (2, 3, 1, 0) for dx in (1, 0) if dx or dz]
    assert len(peers) == 2 * count_col - 1

    def peer_index(dx, dz):
        return dz * 2 + dx - 1

    def place_of(c, freq, col):
        return (c * 2 + freq) * count_col + col

    def focus_copy(b):
        return pltpu.make_async_copy(
            focus_hbm.at[0, :, :, pl.ds(pl.multiple_of(b * TS, TS), TS)], focus_buf.at[b], focus_sem.at[b]
        )

    def v_copy(b):
        return pltpu.make_async_copy(
            v_hbm.at[0, :, :, pl.ds(pl.multiple_of(b * TS, TS), TS)], v_buf.at[b], v_sem.at[b]
        )

    def u_copy(c):
        return pltpu.make_async_copy(u_hbm.at[0, :, 2 * my_freq + c], u_buf.at[c], u_sem.at[c])

    def col_at(dz):
        return lax.rem(my_col + dz, count_col)

    def freq_at(dx):
        return my_freq if dx == 0 else 1 - my_freq

    def device_at(dx, dz):
        return {"freq": freq_at(dx), "col": col_at(dz)}

    def coef_copy(c, dx, dz):
        at = peer_index(dx, dz)
        return pltpu.make_async_remote_copy(
            src_ref=coef_send.at[c, at],
            dst_ref=coef_recv.at[c, my_freq, :, pl.ds(pl.multiple_of(my_col * band, 32), band), :],
            send_sem=coef_send_sem.at[c, at],
            recv_sem=coef_recv_sem.at[c, at],
            device_id=device_at(dx, dz),
            device_id_type=pl.DeviceIdType.MESH,
        )

    def adj_copy(c, dx, dz):
        at = peer_index(dx, dz)
        return pltpu.make_async_remote_copy(
            src_ref=adj_send.at[c, dx, :, pl.ds(pl.multiple_of(col_at(dz) * band, 32), band), :],
            dst_ref=adj_recv.at[place_of(c, my_freq, my_col)],
            send_sem=adj_send_sem.at[c, at],
            recv_sem=adj_recv_sem.at[c, at],
            device_id=device_at(dx, dz),
            device_id_type=pl.DeviceIdType.MESH,
        )

    def far_copy(stage, g):
        c, chunk = divmod(g, CHUNKS)
        grp = 1 - my_grp if stage == 3 else my_grp
        rows = pl.ds(pl.multiple_of((2 * my_rep + grp) * quarter + chunk * piece, 16), piece)
        target = far_u.at[c, :, rows, :]
        source = u_hbm.at[0, :, 2 * (1 - my_freq) + c, rows, :] if stage == 0 else target
        device = ({"freq": 1 - my_freq}, {"grp": 1 - my_grp}, {"rep": 1 - my_rep}, {"rep": 1 - my_rep})[stage]
        return pltpu.make_async_remote_copy(
            src_ref=source,
            dst_ref=target,
            send_sem=far_send_sem.at[stage, g],
            recv_sem=far_recv_sem.at[stage, g],
            device_id=device,
            device_id_type=pl.DeviceIdType.MESH,
        )

    def far_start(c):
        for chunk in range(CHUNKS):
            far_copy(0, c * CHUNKS + chunk).start()

    barrier = pltpu.get_barrier_semaphore()
    for device in [device_at(dx, dz) for dx, dz in peers] + [{"grp": 1 - my_grp}, {"rep": 1 - my_rep}]:
        pl.semaphore_signal(barrier, inc=1, device_id=device, device_id_type=pl.DeviceIdType.MESH)

    for b in range(blocks):
        focus_copy(b).start()
        v_copy(b).start()
    for c in range(ROUNDS):
        u_copy(c).start()

    pl.semaphore_wait(barrier, len(peers) + 2)
    far_start(0)

    dest_of = []
    for tile in range(row_tiles):
        slot = jnp.int32(0)
        for other in range(tile):
            slot = slot + (owners_ref[other] == owners_ref[tile]).astype(jnp.int32)
        dest_of.append(place_of(slot % ROUNDS, slot // ROUNDS, owners_ref[tile]))

    def divided(ids):
        return jnp.right_shift(ids * (-(-65536 // R)), 16)

    column_ids = lax.broadcasted_iota(jnp.int32, (1, ranks_all), 1)
    row_ids = lax.broadcasted_iota(jnp.int32, (places * R, ranks_all), 0)
    column_tile = divided(column_ids)
    column_level = column_ids - column_tile * R
    row_place = divided(row_ids)
    row_level = row_ids - row_place * R
    column_dest = jnp.zeros_like(column_ids)
    for tile in range(row_tiles):
        column_dest = jnp.where(column_tile == tile, dest_of[tile], column_dest)
    routed = (row_place == column_dest) & (row_level == column_level)
    for b in range(blocks):
        column_rank = jnp.zeros_like(column_ids)
        for tile in range(row_tiles):
            column_rank = jnp.where(
                column_tile == tile, ranks_ref[tile, my_col * blocks + b], column_rank
            )
        kept = routed & (row_level < column_rank)
        route_buf[b] = jnp.where(kept, 1.0, 0.0).astype(jnp.bfloat16)

    def partial_step(b, carry):
        focus_copy(b).wait()
        v_copy(b).wait()
        focus_low = focus_buf[b].reshape(2 * vis, TS).astype(jnp.bfloat16)
        products = stacked_dot(v_buf[b].reshape(2 * ranks_all, TS), focus_low, ((1,), (1,)))
        real_part = products[:ranks_all, :vis] - products[ranks_all:, vis:]
        imag_part = products[:ranks_all, vis:] + products[ranks_all:, :vis]
        partials = jnp.concatenate([real_part, imag_part], axis=1).astype(jnp.bfloat16)
        placed = stacked_dot(route_buf[b], partials, ((1,), (0,)))
        part_buf[b, 0] = placed[:, :vis]
        part_buf[b, 1] = placed[:, vis:]
        return carry

    def slot_partials(place, part):
        start = pl.multiple_of(place * R, 8)
        pieces = [part_buf[b, part, pl.ds(start, R), :] for b in range(blocks)]
        return jnp.concatenate(pieces, axis=0).astype(jnp.bfloat16)

    def send_coefs(c, wanted):
        for dx, dz in peers:
            if dx in wanted:
                place = place_of(c, freq_at(dx), col_at(dz))
                for part in range(2):
                    coef_send[c, peer_index(dx, dz), part] = slot_partials(place, part)
                coef_copy(c, dx, dz).start()

    def keep_coefs(c):
        for part in range(2):
            coef_recv[c, my_freq, part, pl.ds(pl.multiple_of(my_col * band, 32), band), :] = slot_partials(
                place_of(c, my_freq, my_col), part
            )

    def await_coefs(c, wanted):
        for dx, dz in peers:
            if dx in wanted:
                coef_copy(c, dx, dz).wait_recv()

    def place_factors(b):
        for part in range(2):
            chosen = stacked_dot(route_buf[b], v_buf[b, part], ((1,), (0,)))
            v_place[b, part] = chosen.astype(jnp.bfloat16)

    def field_of(coef, factors):
        real_coef = coef[0]
        imag_coef = coef[1]
        left_side = jnp.concatenate(
            [
                jnp.concatenate([real_coef, imag_coef], axis=1),
                jnp.concatenate([-imag_coef, real_coef], axis=1),
            ],
            axis=0,
        )
        return stacked_dot(left_side, factors.reshape(2 * ranks_u, TS), ((0,), (0,)))

    def own_field(c):
        u_copy(c).wait()
        field_buf[0] = field_of(coef_recv[c, my_freq], u_buf[c])

    def far_field(c):
        field_buf[1] = field_of(coef_recv[c, 1 - my_freq], far_u[c])

    def window(c):
        place = place_of(c, my_freq, my_col)
        onset_row = jnp.ones((strips, LANES), jnp.int32)
        for tile in range(row_tiles):
            held = onsets_ref[tile * strips : (tile + 1) * strips, :]
            onset_row = jnp.where(dest_of[tile] == place, held, onset_row)
        rows = [window_rows(onset_row, freq_at(dx)) for dx in range(2)]
        for chunk in range(strips):
            lanes = pl.ds(chunk * LANES, LANES)
            cut = slice(chunk, chunk + 1)
            values = [[field_buf[dx, part * vis : (part + 1) * vis, lanes] for part in range(2)] for dx in range(2)]
            for dx in range(2):
                ordered = values[dx] + values[1 - dx]
                for part in range(2):
                    row = rows[dx][part]
                    total = row[0][cut] * ordered[0]
                    for q in range(1, 4):
                        total = total + row[q][cut] * ordered[q]
                    window_buf[dx, part * vis : (part + 1) * vis, lanes] = total.astype(jnp.bfloat16)

    def adjoint(c, dx):
        factors = (u_buf, far_u)[dx][c].reshape(2 * ranks_u, TS)
        products = stacked_dot(factors, window_buf[dx], ((1,), (1,)))
        adj_send[c, dx, 0] = (products[:ranks_u, :vis] + products[ranks_u:, vis:]).astype(jnp.bfloat16)
        adj_send[c, dx, 1] = (products[:ranks_u, vis:] - products[ranks_u:, :vis]).astype(jnp.bfloat16)
        if dx == 0:
            place = place_of(c, my_freq, my_col)
            for part in range(2):
                adj_recv[place, part] = adj_send[c, 0, part, pl.ds(pl.multiple_of(my_col * band, 32), band), :]

    def send_adjoint(c, dx):
        for px, pz in peers:
            if px == dx:
                adj_copy(c, px, pz).start()

    def finish_early():
        for c in range(ROUNDS):
            for dx, dz in peers:
                coef_copy(c, dx, dz).wait_send()
        for dx, dz in peers:
            adj_copy(0, dx, dz).wait_send()
        for stage in range(4):
            for g in range(ROUNDS * CHUNKS):
                far_copy(stage, g).wait_send()

    def gather_side(c, dx):
        for px, pz in peers:
            if px == dx:
                adj_copy(c, px, pz).wait_recv()
        for col in range(count_col):
            place = place_of(c, freq_at(dx), col)
            start = pl.multiple_of(place * R, 8)
            for part in range(2):
                rows = adj_recv[place, part].astype(jnp.float32)
                for b in range(blocks):
                    adj_rows[b, pl.ds(start, R), part * vis : (part + 1) * vis] = rows[b * R : (b + 1) * R]

    def left_of(rows):
        real_adj = rows[:, :vis].astype(jnp.bfloat16)
        imag_adj = rows[:, vis:].astype(jnp.bfloat16)
        return jnp.concatenate(
            [
                jnp.concatenate([real_adj, imag_adj], axis=1),
                jnp.concatenate([imag_adj, -real_adj], axis=1),
            ],
            axis=0,
        )

    def wave_of(b, start, count):
        held = pl.ds(start if isinstance(start, int) else pl.multiple_of(start, 32), count)
        factors = v_place[b, :, held, :].reshape(2 * count, TS)
        return stacked_dot(left_of(adj_rows[b, held, :]), factors, ((0,), (0,))).reshape(2, vis, TS)

    def round_update(b, carry):
        focus_buf[b] = focus_buf[b] - wave_of(b, 0, round_rows)
        return carry

    def side_rows(dx):
        return place_of(1, freq_at(dx), 0) * R

    def side_update(dx):
        def update(b, carry):
            focus_buf[b] = focus_buf[b] - wave_of(b, side_rows(dx), round_rows // 2)
            return carry

        lax.fori_loop(0, blocks, update, 0)

    def hand_over(dx):
        held = pl.ds(pl.multiple_of(side_rows(dx), 32), round_rows // 2)
        for b in range(blocks):
            last_left[b] = left_of(adj_rows[b, held, :])

    def from_freq(g):
        far_copy(0, g).wait_recv()
        far_copy(1, g).start()
        far_copy(2, g).start()

    def from_grp(g):
        far_copy(1, g).wait_recv()
        far_copy(3, g).start()

    def await_far(c):
        for g in range(c * CHUNKS, (c + 1) * CHUNKS):
            far_copy(2, g).wait_recv()
            far_copy(3, g).wait_recv()

    partial_step(0, 0)
    lax.fori_loop(1, blocks, partial_step, 0)
    send_coefs(0, (1,))
    send_coefs(0, (0,))
    far_start(1)
    send_coefs(1, (0,))
    keep_coefs(0)
    keep_coefs(1)
    from_freq(0)
    place_factors(0)
    from_freq(1)
    from_grp(0)
    place_factors(1)
    from_freq(2)
    from_grp(1)
    await_coefs(0, (0,))
    own_field(0)
    from_grp(2)
    from_freq(3)
    await_coefs(0, (1,))
    await_far(0)
    far_field(0)
    window(0)
    send_coefs(1, (1,))
    adjoint(0, 0)
    send_adjoint(0, 0)
    from_freq(4)
    from_grp(3)
    adjoint(0, 1)
    place_factors(2)
    place_factors(3)
    from_freq(5)
    from_grp(4)
    send_adjoint(0, 1)
    await_coefs(1, (0,))
    own_field(1)
    from_grp(5)
    await_coefs(1, (1,))
    await_far(1)
    far_field(1)
    window(1)
    adjoint(1, 1)
    send_adjoint(1, 1)
    adjoint(1, 0)
    send_adjoint(1, 0)
    gather_side(0, 0)
    gather_side(0, 1)
    lax.fori_loop(0, blocks, round_update, 0)
    finish_early()
    gather_side(1, 1)
    side_update(1)
    gather_side(1, 0)
    hand_over(0)

    for dx, dz in peers:
        adj_copy(1, dx, dz).wait_send()


def last_kernel(focus_ref, factors_ref, left_ref, out_hbm, out_buf, out_sem):
    blocks = focus_ref.shape[0]
    count = left_ref.shape[1] // 2
    start = pl.multiple_of((2 + lax.axis_index("freq")) * count, 32)

    def out_copy(b):
        return pltpu.make_async_copy(
            out_buf.at[b], out_hbm.at[0, :, :, pl.ds(b * TS, TS)], out_sem.at[b]
        )

    for b in range(blocks):
        factors = factors_ref[b, :, pl.ds(start, count), :].reshape(2 * count, TS)
        wave = stacked_dot(left_ref[b], factors, ((0,), (0,)))
        out_buf[b] = focus_ref[b] - wave.reshape(out_buf.shape[1:])
        out_copy(b).start()
    for b in range(blocks):
        out_copy(b).wait()


def fused_device(focusing, v_factors, u_factors, tile_ranks, owners, onsets):
    count_col = lax.axis_size("col")
    vis = focusing.shape[2]
    sources_dev = focusing.shape[3]
    blocks = sources_dev // TS
    ranks_all = (NR // TS) * R
    ranks_u = (NS // TS) * R
    band = blocks * R
    low = jnp.bfloat16
    peers = 2 * count_col - 1
    places = 2 * ROUNDS * count_col
    dma = pltpu.SemaphoreType.DMA
    scratch = [
        pltpu.VMEM((blocks, 2, ranks_all, TS), low),
        pltpu.VMEM((ROUNDS, 2, ranks_u, TS), low),
        pltpu.VMEM((ROUNDS, 2, ranks_u, TS), low),
        pltpu.VMEM((blocks, 2, places * R, vis), jnp.float32),
        pltpu.VMEM((ROUNDS, peers, 2, band, vis), low),
        pltpu.VMEM((ROUNDS, 2, 2, ranks_u, vis), low),
        pltpu.VMEM((2, 2 * vis, TS), jnp.float32),
        pltpu.VMEM((2, 2 * vis, TS), low),
        pltpu.VMEM((ROUNDS, 2, 2, ranks_u, vis), low),
        pltpu.VMEM((places, 2, band, vis), low),
        pltpu.VMEM((blocks, places * R, 2 * vis), jnp.float32),
        pltpu.VMEM((blocks, places * R, ranks_all), low),
        dma((blocks,)),
        dma((blocks,)),
        dma((ROUNDS,)),
        dma((ROUNDS, peers)),
        dma((ROUNDS, peers)),
        dma((ROUNDS, peers)),
        dma((ROUNDS, peers)),
        dma((4, ROUNDS * CHUNKS)),
        dma((4, ROUNDS * CHUNKS)),
    ]
    handed = [
        pltpu.VMEM((blocks, 2, vis, TS), jnp.float32),
        pltpu.VMEM((blocks, 2, places * R, TS), low),
        pltpu.VMEM((blocks, 2 * count_col * R, 2 * vis), low),
    ]
    held = pl.BlockSpec(memory_space=pltpu.VMEM)
    passed = pl.pallas_call(
        functools.partial(fused_kernel, count_col),
        out_shape=handed,
        in_specs=[
            pl.BlockSpec(memory_space=pltpu.SMEM),
            pl.BlockSpec(memory_space=pltpu.SMEM),
            pl.BlockSpec(memory_space=pltpu.VMEM),
            pl.BlockSpec(memory_space=pl.ANY),
            pl.BlockSpec(memory_space=pl.ANY),
            pl.BlockSpec(memory_space=pl.ANY),
        ],
        out_specs=[held] * 3,
        scratch_shapes=scratch,
        compiler_params=pltpu.CompilerParams(
            collective_id=0, has_side_effects=True, vmem_limit_bytes=FIRST_VMEM * 1024 * 1024
        ),
        name="marchenko",
    )(owners, tile_ranks, onsets.reshape(NR // LANES, LANES), focusing, v_factors, u_factors)
    return pl.pallas_call(
        last_kernel,
        out_shape=jax.ShapeDtypeStruct(focusing.shape, jnp.float32),
        in_specs=[held] * 3,
        out_specs=pl.BlockSpec(memory_space=pl.ANY),
        scratch_shapes=[pltpu.VMEM((blocks, 2, vis, TS), jnp.float32), dma((blocks,))],
        compiler_params=pltpu.CompilerParams(vmem_limit_bytes=8 * 1024 * 1024),
        name="last_update",
    )(*passed)


def choose(focusing, v_factors, u_factors, tile_ranks, owners, onsets):
    whole_blocks = focusing.shape[3] % TS == 0
    paired = lax.axis_size("freq") == 2 and focusing.shape[0] == 1
    replicas = lax.axis_size("grp") == 2 and lax.axis_size("rep") == 2
    slots = u_factors.shape[2] == 2 * ROUNDS and lax.axis_size("col") == 4
    program = fused_device if whole_blocks and paired and replicas and slots else per_device
    return program(focusing, v_factors, u_factors, tile_ranks, owners, onsets)


def solution(mesh):
    return jax.shard_map(
        choose,
        mesh=mesh,
        in_specs=(
            P("freq", None, ("grp", "rep"), "col"),
            P("freq", None, None, "col"),
            P("freq", None, "col", None, None),
            P(),
            P(),
            P(),
        ),
        out_specs=P("freq", None, ("grp", "rep"), "col"),
        check_vma=False,
    )
```

```python
import functools
import math

import jax
import jax.numpy as jnp
from jax import lax
from jax.experimental import pallas as pl
from jax.experimental.pallas import tpu as pltpu
from jax.sharding import PartitionSpec as P

TS = 1024
R = 24
NR = 16384
NS = 16384
NT = 512
KLO = 8
LANES = 128
ROUNDS = 2
CHUNKS = 3
ORDER = (2, 3, 1, 0)
FIRST_VMEM = 50


def window_tables(count_freq, onset_rows):
    time_steps = jnp.arange(NT, dtype=jnp.int32)
    freq_bins = KLO + jnp.arange(count_freq, dtype=jnp.int32)
    phases = 2.0 * jnp.pi * (freq_bins[None, :] * time_steps[:, None] % NT).astype(jnp.float32) / NT
    cosine = jnp.cos(phases)
    sines = jnp.sin(phases)
    analyse = jnp.stack([cosine, -sines], axis=2).reshape(NT, 2 * count_freq)
    synthesis = analyse * (2.0 / NT)
    product_table = (analyse[:, :, None] * synthesis[:, None, :]).reshape(
        NT, 4 * count_freq * count_freq
    )
    lower = (time_steps[:, None] >= time_steps[None, :]).astype(jnp.float32)
    running_table = jnp.dot(lower, product_table, precision=lax.Precision.HIGHEST)
    mixing = jnp.take(running_table, onset_rows - 1, axis=0)
    return mixing.reshape(-1, 2 * count_freq, 2 * count_freq)


def kernel_product(einsum_recipe, left_side, right_side):
    return jnp.einsum(einsum_recipe, left_side, right_side, preferred_element_type=jnp.float32)


def per_device(focusing, v_factors, u_factors, tile_ranks, owners, onsets):
    count_col = lax.axis_size("col")
    my_column = lax.axis_index("col")
    count_freq = lax.axis_size("freq")
    my_freq = lax.axis_index("freq")
    freq_dev = focusing.shape[0]
    vis_dev = focusing.shape[2]
    sources_dev = focusing.shape[3]
    capacity = u_factors.shape[2]
    block_width = min(sources_dev, TS)
    blocks_dev = sources_dev // block_width
    per_tile = TS // block_width
    all_blocks = count_col * blocks_dev
    row_tiles = NR // TS
    col_tiles = NS // TS
    freq_all = freq_dev * count_freq
    quarter = TS // count_freq
    tile_ids = jnp.arange(row_tiles, dtype=jnp.int32)
    same_owner = owners[:, None] == owners[None, :]
    earlier = tile_ids[None, :] < tile_ids[:, None]
    slot_of = jnp.sum((same_owner & earlier).astype(jnp.int32), axis=1)
    slot_ids = jnp.arange(capacity, dtype=jnp.int32)
    routing = (owners[None, None, :] == jnp.arange(count_col, dtype=jnp.int32)[:, None, None]) & (
        slot_of[None, None, :] == slot_ids[None, :, None]
    )
    lower_routing = routing.astype(jnp.bfloat16)
    my_slots = ((owners[None, :] == my_column) & (slot_of[None, :] == slot_ids[:, None])).astype(
        jnp.int32
    )
    slot_ranks = jnp.sum(my_slots[:, :, None] * tile_ranks[None, :, :], axis=1)
    rank_mask = (jnp.arange(R, dtype=jnp.int32)[None, None, :] < slot_ranks[:, :, None]).astype(
        jnp.float32
    )
    slot_onsets = jnp.sum(my_slots[:, :, None] * onsets.reshape(row_tiles, TS)[None], axis=1)
    slot_onsets = jnp.maximum(slot_onsets, 1)
    focus_low = focusing.astype(jnp.bfloat16).reshape(freq_dev, 2, vis_dev, blocks_dev, block_width)
    factors_v = v_factors.reshape(freq_dev, 2, row_tiles, R, blocks_dev, block_width)
    einsum_recipe = "fikbs,fvbs->ifbkv"
    real_portion = kernel_product(einsum_recipe, factors_v[:, 0], focus_low[:, 0]) - kernel_product(
        einsum_recipe, factors_v[:, 1], focus_low[:, 1]
    )
    part_imag = kernel_product(einsum_recipe, factors_v[:, 0], focus_low[:, 1]) + kernel_product(
        einsum_recipe, factors_v[:, 1], focus_low[:, 0]
    )
    partial_sums = jnp.stack([real_portion, part_imag], axis=3).astype(jnp.bfloat16)
    outgoing_parts = kernel_product("way,ymleno->amwleno", lower_routing, partial_sums).astype(
        jnp.bfloat16
    )
    outgoing_parts = outgoing_parts.reshape(capacity, freq_dev, all_blocks, 2, R, vis_dev)
    arrived = lax.all_to_all(outgoing_parts, "col", split_axis=2, concat_axis=2, tiled=True)
    coefficients = jnp.sum(
        arrived.astype(jnp.float32).reshape(capacity, freq_dev, col_tiles, per_tile, 2, R, vis_dev),
        axis=3,
    )
    coefficients = (coefficients * rank_mask[:, None, :, None, :, None]).astype(jnp.bfloat16)
    factors_u = u_factors.reshape(freq_dev, 2, capacity, col_tiles, R, TS)
    uform = "fcjka,cfjkv->cfav"
    field_real = kernel_product(uform, factors_u[:, 0], coefficients[:, :, :, 0]) - kernel_product(
        uform, factors_u[:, 1], coefficients[:, :, :, 1]
    )
    field_imag = kernel_product(uform, factors_u[:, 0], coefficients[:, :, :, 1]) + kernel_product(
        uform, factors_u[:, 1], coefficients[:, :, :, 0]
    )
    receiver_field = jnp.stack([field_real, field_imag], axis=2).astype(jnp.bfloat16)
    turned = lax.all_to_all(receiver_field, "freq", split_axis=3, concat_axis=1, tiled=True)
    quarter_onsets = lax.dynamic_slice_in_dim(slot_onsets, my_freq * quarter, quarter, 1)
    mixing = window_tables(freq_all, quarter_onsets.reshape(-1)).reshape(
        capacity, quarter, 2 * freq_all, 2 * freq_all
    )
    flat_field = turned.reshape(capacity, 2 * freq_all, quarter, vis_dev).astype(jnp.float32)
    mixed_field = jnp.einsum("crpq,cqrv->cprv", mixing, flat_field, precision=lax.Precision.HIGHEST)
    mixed_field = mixed_field.astype(jnp.bfloat16).reshape(capacity, freq_all, 2, quarter, vis_dev)
    windowed = lax.all_to_all(mixed_field, "freq", split_axis=1, concat_axis=3, tiled=True)
    aform = "fcjka,cfav->cfjkv"
    back_real = kernel_product(aform, factors_u[:, 0], windowed[:, :, 0]) + kernel_product(
        aform, factors_u[:, 1], windowed[:, :, 1]
    )
    back_imag = kernel_product(aform, factors_u[:, 0], windowed[:, :, 1]) - kernel_product(
        aform, factors_u[:, 1], windowed[:, :, 0]
    )
    adjoint = jnp.stack([back_real, back_imag], axis=3) * rank_mask[:, None, :, None, :, None]
    adjoint = adjoint.astype(jnp.bfloat16)
    spread = jnp.broadcast_to(
        adjoint[:, :, :, None], (capacity, freq_dev, col_tiles, per_tile, 2, R, vis_dev)
    )
    spread = spread.reshape(capacity, freq_dev, all_blocks, 2, R, vis_dev)
    result_field = lax.all_to_all(spread, "col", split_axis=2, concat_axis=2, tiled=True)
    result_field = result_field.reshape(capacity, freq_dev, count_col, blocks_dev, 2, R, vis_dev)
    row_share = kernel_product("prq,rjpagwu->qjagwu", lower_routing, result_field).astype(
        jnp.bfloat16
    )
    wform = "fikbs,ifbkv->fvbs"
    wave_real = kernel_product(wform, factors_v[:, 0], row_share[:, :, :, 0]) + kernel_product(
        wform, factors_v[:, 1], row_share[:, :, :, 1]
    )
    wave_imag = kernel_product(wform, factors_v[:, 0], row_share[:, :, :, 1]) - kernel_product(
        wform, factors_v[:, 1], row_share[:, :, :, 0]
    )
    wave_field = jnp.stack([wave_real, wave_imag], axis=1).reshape(
        freq_dev, 2, vis_dev, sources_dev
    )
    return focusing - wave_field


def window_rows(onset_row, my_freq):
    sign = (2 * my_freq - 1).astype(jnp.float32)

    def sums(bins, inverse):
        phase_all = jnp.bitwise_and(bins * onset_row, 2 * NT - 1).astype(jnp.float32) * (math.pi / NT)
        phase_less = jnp.bitwise_and(bins * (onset_row - 1), 2 * NT - 1).astype(jnp.float32) * (math.pi / NT)
        scaled = jnp.sin(phase_all) * inverse
        return jnp.cos(phase_less) * scaled, jnp.sin(phase_less) * scaled

    def inverse_of(bins):
        return 1.0 / (NT * math.sin(math.pi * bins / NT))

    own_inverse = jnp.where(my_freq == 0, inverse_of(2 * KLO), inverse_of(2 * KLO + 2))
    own_cos, own_sin = sums(2 * KLO + 2 * my_freq, own_inverse)
    sum_cos, sum_sin = sums(2 * KLO + 1, inverse_of(2 * KLO + 1))
    gap_cos, gap_sin = sums(1, inverse_of(1))
    level = onset_row.astype(jnp.float32) * (1.0 / NT)
    real_row = (level + own_cos, -own_sin, gap_cos + sum_cos, sign * gap_sin - sum_sin)
    imag_row = (-own_sin, level - own_cos, -sum_sin - sign * gap_sin, gap_cos - sum_cos)
    return real_row, imag_row


def stacked_dot(left_side, right_side, dims):
    return lax.dot_general(left_side, right_side, (dims, ((), ())), preferred_element_type=jnp.float32)


def fused_kernel(
    count_col,
    owners_ref,
    ranks_ref,
    onsets_ref,
    focus_hbm,
    v_hbm,
    u_hbm,
    focus_buf,
    v_place,
    last_left,
    v_buf,
    u_buf,
    far_u,
    part_buf,
    coef_send,
    coef_recv,
    field_buf,
    window_buf,
    table_buf,
    adj_send,
    adj_recv,
    adj_rows,
    route_buf,
    focus_sem,
    v_sem,
    u_sem,
    coef_send_sem,
    coef_recv_sem,
    adj_send_sem,
    adj_recv_sem,
    far_send_sem,
    far_recv_sem,
):
    my_col = lax.axis_index("col")
    my_freq = lax.axis_index("freq")
    my_grp = lax.axis_index("grp")
    my_rep = lax.axis_index("rep")
    blocks = focus_buf.shape[0]
    vis = focus_buf.shape[2]
    row_tiles = NR // TS
    col_tiles = NS // TS
    band = blocks * R
    ranks_all = row_tiles * R
    ranks_u = col_tiles * R
    strips = TS // LANES
    quarter = ranks_u // 4
    piece = quarter // CHUNKS
    places = 2 * ROUNDS * count_col
    round_rows = 2 * count_col * R
    peers = [(dx, dz) for dz in ORDER for dx in (1, 0) if dx or dz]
    assert len(peers) == 2 * count_col - 1

    def peer_index(dx, dz):
        return dz * 2 + dx - 1

    def place_of(c, freq, col):
        return (c * 2 + freq) * count_col + col

    def focus_copy(b):
        return pltpu.make_async_copy(
            focus_hbm.at[0, :, :, pl.ds(pl.multiple_of(b * TS, TS), TS)], focus_buf.at[b], focus_sem.at[b]
        )

    def v_copy(b):
        return pltpu.make_async_copy(
            v_hbm.at[0, :, :, pl.ds(pl.multiple_of(b * TS, TS), TS)], v_buf.at[b], v_sem.at[b]
        )

    def u_copy(c):
        return pltpu.make_async_copy(u_hbm.at[0, :, 2 * my_freq + c], u_buf.at[c], u_sem.at[c])

    def col_at(dz):
        return lax.rem(my_col + dz, count_col)

    def freq_at(dx):
        return my_freq if dx == 0 else 1 - my_freq

    def device_at(dx, dz):
        return {"freq": freq_at(dx), "col": col_at(dz)}

    def coef_copy(c, dx, dz):
        at = peer_index(dx, dz)
        return pltpu.make_async_remote_copy(
            src_ref=coef_send.at[c, at],
            dst_ref=coef_recv.at[c, my_freq, :, pl.ds(pl.multiple_of(my_col * band, 32), band), :],
            send_sem=coef_send_sem.at[c, at],
            recv_sem=coef_recv_sem.at[c, at],
            device_id=device_at(dx, dz),
            device_id_type=pl.DeviceIdType.MESH,
        )

    def adj_copy(c, dx, dz):
        at = peer_index(dx, dz)
        return pltpu.make_async_remote_copy(
            src_ref=adj_send.at[c, dx, :, pl.ds(pl.multiple_of(col_at(dz) * band, 32), band), :],
            dst_ref=adj_recv.at[place_of(c, my_freq, my_col)],
            send_sem=adj_send_sem.at[c, at],
            recv_sem=adj_recv_sem.at[c, at],
            device_id=device_at(dx, dz),
            device_id_type=pl.DeviceIdType.MESH,
        )

    def far_copy(stage, g):
        c, chunk = divmod(g, CHUNKS)
        grp = 1 - my_grp if stage == 3 else my_grp
        rows = pl.ds(pl.multiple_of((2 * my_rep + grp) * quarter + chunk * piece, 16), piece)
        target = far_u.at[c, :, rows, :]
        source = u_hbm.at[0, :, 2 * (1 - my_freq) + c, rows, :] if stage == 0 else target
        device = ({"freq": 1 - my_freq}, {"grp": 1 - my_grp}, {"rep": 1 - my_rep}, {"rep": 1 - my_rep})[stage]
        return pltpu.make_async_remote_copy(
            src_ref=source,
            dst_ref=target,
            send_sem=far_send_sem.at[stage, g],
            recv_sem=far_recv_sem.at[stage, g],
            device_id=device,
            device_id_type=pl.DeviceIdType.MESH,
        )

    def far_start(c):
        for chunk in range(CHUNKS):
            far_copy(0, c * CHUNKS + chunk).start()

    barrier = pltpu.get_barrier_semaphore()
    for device in [device_at(dx, dz) for dx, dz in peers] + [{"grp": 1 - my_grp}, {"rep": 1 - my_rep}]:
        pl.semaphore_signal(barrier, inc=1, device_id=device, device_id_type=pl.DeviceIdType.MESH)

    for b in range(blocks):
        focus_copy(b).start()
        v_copy(b).start()
    for c in range(ROUNDS):
        u_copy(c).start()

    pl.semaphore_wait(barrier, len(peers) + 2)
    far_start(0)

    dest_of = []
    for tile in range(row_tiles):
        slot = jnp.int32(0)
        for other in range(tile):
            slot = slot + (owners_ref[other] == owners_ref[tile]).astype(jnp.int32)
        dest_of.append(place_of(slot % ROUNDS, slot // ROUNDS, owners_ref[tile]))

    def divided(ids):
        return jnp.right_shift(ids * (-(-65536 // R)), 16)

    column_ids = lax.broadcasted_iota(jnp.int32, (1, ranks_all), 1)
    row_ids = lax.broadcasted_iota(jnp.int32, (places * R, ranks_all), 0)
    column_tile = divided(column_ids)
    column_level = column_ids - column_tile * R
    row_place = divided(row_ids)
    row_level = row_ids - row_place * R
    column_dest = jnp.zeros_like(column_ids)
    for tile in range(row_tiles):
        column_dest = jnp.where(column_tile == tile, dest_of[tile], column_dest)
    routed = (row_place == column_dest) & (row_level == column_level)
    for b in range(blocks):
        column_rank = jnp.zeros_like(column_ids)
        for tile in range(row_tiles):
            column_rank = jnp.where(
                column_tile == tile, ranks_ref[tile, my_col * blocks + b], column_rank
            )
        kept = routed & (row_level < column_rank)
        route_buf[b] = jnp.where(kept, 1.0, 0.0).astype(jnp.bfloat16)

    def partial_step(b, carry):
        focus_copy(b).wait()
        v_copy(b).wait()
        focus_low = focus_buf[b].reshape(2 * vis, TS).astype(jnp.bfloat16)
        products = stacked_dot(v_buf[b].reshape(2 * ranks_all, TS), focus_low, ((1,), (1,)))
        real_part = products[:ranks_all, :vis] - products[ranks_all:, vis:]
        imag_part = products[:ranks_all, vis:] + products[ranks_all:, :vis]
        partials = jnp.concatenate([real_part, imag_part], axis=1).astype(jnp.bfloat16)
        placed = stacked_dot(route_buf[b], partials, ((1,), (0,)))
        part_buf[b, 0] = placed[:, :vis]
        part_buf[b, 1] = placed[:, vis:]
        return carry

    def slot_partials(place, part):
        start = pl.multiple_of(place * R, 8)
        pieces = [part_buf[b, part, pl.ds(start, R), :] for b in range(blocks)]
        return jnp.concatenate(pieces, axis=0).astype(jnp.bfloat16)

    def send_coefs(c, wanted):
        for dx, dz in peers:
            if dx in wanted:
                place = place_of(c, freq_at(dx), col_at(dz))
                for part in range(2):
                    coef_send[c, peer_index(dx, dz), part] = slot_partials(place, part)
                coef_copy(c, dx, dz).start()

    def keep_coefs(c):
        for part in range(2):
            coef_recv[c, my_freq, part, pl.ds(pl.multiple_of(my_col * band, 32), band), :] = slot_partials(
                place_of(c, my_freq, my_col), part
            )

    def await_coefs(c, wanted):
        for dx, dz in peers:
            if dx in wanted:
                coef_copy(c, dx, dz).wait_recv()

    def place_factors(b):
        for part in range(2):
            chosen = stacked_dot(route_buf[b], v_buf[b, part], ((1,), (0,)))
            v_place[b, part] = chosen.astype(jnp.bfloat16)

    def field_of(coef, factors):
        real_coef = coef[0]
        imag_coef = coef[1]
        left_side = jnp.concatenate(
            [
                jnp.concatenate([real_coef, imag_coef], axis=1),
                jnp.concatenate([-imag_coef, real_coef], axis=1),
            ],
            axis=0,
        )
        return stacked_dot(left_side, factors.reshape(2 * ranks_u, TS), ((0,), (0,)))

    def own_field(c):
        u_copy(c).wait()
        field_buf[0] = field_of(coef_recv[c, my_freq], u_buf[c])

    def far_field(c):
        field_buf[1] = field_of(coef_recv[c, 1 - my_freq], far_u[c])

    def window_table(c):
        place = place_of(c, my_freq, my_col)
        onset_row = jnp.ones((strips, LANES), jnp.int32)
        for tile in range(row_tiles):
            held = onsets_ref[tile * strips : (tile + 1) * strips, :]
            onset_row = jnp.where(dest_of[tile] == place, held, onset_row)
        for dx in range(2):
            for part, rows in enumerate(window_rows(onset_row, freq_at(dx))):
                for q in range(4):
                    table_buf[c, dx, part, q] = rows[q]

    def window(c, dx):
        for chunk in range(strips):
            lanes = pl.ds(chunk * LANES, LANES)
            ordered = [
                field_buf[side, part * vis : (part + 1) * vis, lanes] for side in (dx, 1 - dx) for part in range(2)
            ]
            for part in range(2):
                total = table_buf[c, dx, part, 0, chunk : chunk + 1] * ordered[0]
                for q in range(1, 4):
                    total = total + table_buf[c, dx, part, q, chunk : chunk + 1] * ordered[q]
                window_buf[dx, part * vis : (part + 1) * vis, lanes] = total.astype(jnp.bfloat16)

    def adjoint(c, dx):
        factors = (u_buf, far_u)[dx][c].reshape(2 * ranks_u, TS)
        products = stacked_dot(factors, window_buf[dx], ((1,), (1,)))
        adj_send[c, dx, 0] = (products[:ranks_u, :vis] + products[ranks_u:, vis:]).astype(jnp.bfloat16)
        adj_send[c, dx, 1] = (products[:ranks_u, vis:] - products[ranks_u:, :vis]).astype(jnp.bfloat16)
        if dx == 0:
            place = place_of(c, my_freq, my_col)
            for part in range(2):
                adj_recv[place, part] = adj_send[c, 0, part, pl.ds(pl.multiple_of(my_col * band, 32), band), :]

    def send_adjoint(c, dx):
        for px, pz in peers:
            if px == dx:
                adj_copy(c, px, pz).start()

    def finish_early():
        for c in range(ROUNDS):
            for dx, dz in peers:
                coef_copy(c, dx, dz).wait_send()
        for dx, dz in peers:
            adj_copy(0, dx, dz).wait_send()
        for stage in range(4):
            for g in range(ROUNDS * CHUNKS):
                far_copy(stage, g).wait_send()

    def gather_side(c, dx):
        for px, pz in peers:
            if px == dx:
                adj_copy(c, px, pz).wait_recv()
        for col in range(count_col):
            place = place_of(c, freq_at(dx), col)
            start = pl.multiple_of(place * R, 8)
            for part in range(2):
                rows = adj_recv[place, part].astype(jnp.float32)
                for b in range(blocks):
                    adj_rows[b, pl.ds(start, R), part * vis : (part + 1) * vis] = rows[b * R : (b + 1) * R]

    def left_of(rows):
        real_adj = rows[:, :vis].astype(jnp.bfloat16)
        imag_adj = rows[:, vis:].astype(jnp.bfloat16)
        return jnp.concatenate(
            [
                jnp.concatenate([real_adj, imag_adj], axis=1),
                jnp.concatenate([imag_adj, -real_adj], axis=1),
            ],
            axis=0,
        )

    def wave_of(b, start, count):
        held = pl.ds(start if isinstance(start, int) else pl.multiple_of(start, 32), count)
        factors = v_place[b, :, held, :].reshape(2 * count, TS)
        return stacked_dot(left_of(adj_rows[b, held, :]), factors, ((0,), (0,))).reshape(2, vis, TS)

    def round_update(b, carry):
        focus_buf[b] = focus_buf[b] - wave_of(b, 0, round_rows)
        return carry

    def side_rows(dx):
        return place_of(1, freq_at(dx), 0) * R

    def side_update(dx):
        def update(b, carry):
            focus_buf[b] = focus_buf[b] - wave_of(b, side_rows(dx), round_rows // 2)
            return carry

        lax.fori_loop(0, blocks, update, 0)

    def hand_over(dx):
        held = pl.ds(pl.multiple_of(side_rows(dx), 32), round_rows // 2)
        for b in range(blocks):
            last_left[b] = left_of(adj_rows[b, held, :])

    def from_freq(g):
        far_copy(0, g).wait_recv()
        far_copy(1, g).start()
        far_copy(2, g).start()

    def from_grp(g):
        far_copy(1, g).wait_recv()
        far_copy(3, g).start()

    def await_far(c):
        for g in range(c * CHUNKS, (c + 1) * CHUNKS):
            far_copy(2, g).wait_recv()
            far_copy(3, g).wait_recv()

    partial_step(0, 0)
    lax.fori_loop(1, blocks, partial_step, 0)
    send_coefs(0, (1,))
    far_start(1)
    send_coefs(0, (0,))
    send_coefs(1, (0,))
    keep_coefs(0)
    keep_coefs(1)
    from_freq(0)
    place_factors(0)
    window_table(0)
    from_freq(1)
    from_grp(0)
    place_factors(1)
    window_table(1)
    from_freq(2)
    from_grp(1)
    await_coefs(0, (0,))
    own_field(0)
    from_grp(2)
    from_freq(3)
    await_coefs(0, (1,))
    await_far(0)
    far_field(0)
    send_coefs(1, (1,))
    window(0, 0)
    adjoint(0, 0)
    send_adjoint(0, 0)
    from_freq(4)
    from_grp(3)
    window(0, 1)
    adjoint(0, 1)
    place_factors(2)
    place_factors(3)
    from_freq(5)
    from_grp(4)
    send_adjoint(0, 1)
    await_coefs(1, (0,))
    own_field(1)
    from_grp(5)
    await_coefs(1, (1,))
    await_far(1)
    far_field(1)
    window(1, 1)
    adjoint(1, 1)
    send_adjoint(1, 1)
    window(1, 0)
    adjoint(1, 0)
    send_adjoint(1, 0)
    gather_side(0, 0)
    gather_side(0, 1)
    lax.fori_loop(0, blocks, round_update, 0)
    finish_early()
    gather_side(1, 1)
    side_update(1)
    gather_side(1, 0)
    hand_over(0)

    for dx, dz in peers:
        adj_copy(1, dx, dz).wait_send()


def last_kernel(focus_ref, factors_ref, left_ref, out_hbm, out_buf, out_sem):
    blocks = focus_ref.shape[0]
    count = left_ref.shape[1] // 2
    start = pl.multiple_of((2 + lax.axis_index("freq")) * count, 32)

    def out_copy(b):
        return pltpu.make_async_copy(
            out_buf.at[b], out_hbm.at[0, :, :, pl.ds(b * TS, TS)], out_sem.at[b]
        )

    for b in range(blocks):
        factors = factors_ref[b, :, pl.ds(start, count), :].reshape(2 * count, TS)
        wave = stacked_dot(left_ref[b], factors, ((0,), (0,)))
        out_buf[b] = focus_ref[b] - wave.reshape(out_buf.shape[1:])
        out_copy(b).start()
    for b in range(blocks):
        out_copy(b).wait()


def fused_device(focusing, v_factors, u_factors, tile_ranks, owners, onsets):
    count_col = lax.axis_size("col")
    vis = focusing.shape[2]
    sources_dev = focusing.shape[3]
    blocks = sources_dev // TS
    ranks_all = (NR // TS) * R
    ranks_u = (NS // TS) * R
    band = blocks * R
    low = jnp.bfloat16
    peers = 2 * count_col - 1
    places = 2 * ROUNDS * count_col
    dma = pltpu.SemaphoreType.DMA
    scratch = [
        pltpu.VMEM((blocks, 2, ranks_all, TS), low),
        pltpu.VMEM((ROUNDS, 2, ranks_u, TS), low),
        pltpu.VMEM((ROUNDS, 2, ranks_u, TS), low),
        pltpu.VMEM((blocks, 2, places * R, vis), jnp.float32),
        pltpu.VMEM((ROUNDS, peers, 2, band, vis), low),
        pltpu.VMEM((ROUNDS, 2, 2, ranks_u, vis), low),
        pltpu.VMEM((2, 2 * vis, TS), jnp.float32),
        pltpu.VMEM((2, 2 * vis, TS), low),
        pltpu.VMEM((ROUNDS, 2, 2, 4, TS // LANES, LANES), jnp.float32),
        pltpu.VMEM((ROUNDS, 2, 2, ranks_u, vis), low),
        pltpu.VMEM((places, 2, band, vis), low),
        pltpu.VMEM((blocks, places * R, 2 * vis), jnp.float32),
        pltpu.VMEM((blocks, places * R, ranks_all), low),
        dma((blocks,)),
        dma((blocks,)),
        dma((ROUNDS,)),
        dma((ROUNDS, peers)),
        dma((ROUNDS, peers)),
        dma((ROUNDS, peers)),
        dma((ROUNDS, peers)),
        dma((4, ROUNDS * CHUNKS)),
        dma((4, ROUNDS * CHUNKS)),
    ]
    handed = [
        pltpu.VMEM((blocks, 2, vis, TS), jnp.float32),
        pltpu.VMEM((blocks, 2, places * R, TS), low),
        pltpu.VMEM((blocks, 2 * count_col * R, 2 * vis), low),
    ]
    held = pl.BlockSpec(memory_space=pltpu.VMEM)
    passed = pl.pallas_call(
        functools.partial(fused_kernel, count_col),
        out_shape=handed,
        in_specs=[
            pl.BlockSpec(memory_space=pltpu.SMEM),
            pl.BlockSpec(memory_space=pltpu.SMEM),
            pl.BlockSpec(memory_space=pltpu.VMEM),
            pl.BlockSpec(memory_space=pl.ANY),
            pl.BlockSpec(memory_space=pl.ANY),
            pl.BlockSpec(memory_space=pl.ANY),
        ],
        out_specs=[held] * 3,
        scratch_shapes=scratch,
        compiler_params=pltpu.CompilerParams(
            collective_id=0, has_side_effects=True, vmem_limit_bytes=FIRST_VMEM * 1024 * 1024
        ),
        name="marchenko",
    )(owners, tile_ranks, onsets.reshape(NR // LANES, LANES), focusing, v_factors, u_factors)
    return pl.pallas_call(
        last_kernel,
        out_shape=jax.ShapeDtypeStruct(focusing.shape, jnp.float32),
        in_specs=[held] * 3,
        out_specs=pl.BlockSpec(memory_space=pl.ANY),
        scratch_shapes=[pltpu.VMEM((blocks, 2, vis, TS), jnp.float32), dma((blocks,))],
        compiler_params=pltpu.CompilerParams(vmem_limit_bytes=8 * 1024 * 1024),
        name="last_update",
    )(*passed)


def choose(focusing, v_factors, u_factors, tile_ranks, owners, onsets):
    whole_blocks = focusing.shape[3] % TS == 0
    paired = lax.axis_size("freq") == 2 and focusing.shape[0] == 1
    replicas = lax.axis_size("grp") == 2 and lax.axis_size("rep") == 2
    slots = u_factors.shape[2] == 2 * ROUNDS and lax.axis_size("col") == 4
    program = fused_device if whole_blocks and paired and replicas and slots else per_device
    return program(focusing, v_factors, u_factors, tile_ranks, owners, onsets)


def solution(mesh):
    return jax.shard_map(
        choose,
        mesh=mesh,
        in_specs=(
            P("freq", None, ("grp", "rep"), "col"),
            P("freq", None, None, "col"),
            P("freq", None, "col", None, None),
            P(),
            P(),
            P(),
        ),
        out_specs=P("freq", None, ("grp", "rep"), "col"),
        check_vma=False,
    )
```

```python
import functools
import math

import jax
import jax.numpy as jnp
from jax import lax
from jax.experimental import pallas as pl
from jax.experimental.pallas import tpu as pltpu
from jax.sharding import PartitionSpec as P

TS = 1024
R = 24
NR = 16384
NS = 16384
NT = 512
KLO = 8
LANES = 128
ROUNDS = 2
CHUNKS = 3
ORDER = (2, 3, 1, 0)
FIRST_VMEM = 50


def window_tables(count_freq, onset_rows):
    time_steps = jnp.arange(NT, dtype=jnp.int32)
    freq_bins = KLO + jnp.arange(count_freq, dtype=jnp.int32)
    phases = 2.0 * jnp.pi * (freq_bins[None, :] * time_steps[:, None] % NT).astype(jnp.float32) / NT
    cosine = jnp.cos(phases)
    sines = jnp.sin(phases)
    analyse = jnp.stack([cosine, -sines], axis=2).reshape(NT, 2 * count_freq)
    synthesis = analyse * (2.0 / NT)
    product_table = (analyse[:, :, None] * synthesis[:, None, :]).reshape(
        NT, 4 * count_freq * count_freq
    )
    lower = (time_steps[:, None] >= time_steps[None, :]).astype(jnp.float32)
    running_table = jnp.dot(lower, product_table, precision=lax.Precision.HIGHEST)
    mixing = jnp.take(running_table, onset_rows - 1, axis=0)
    return mixing.reshape(-1, 2 * count_freq, 2 * count_freq)


def kernel_product(einsum_recipe, left_side, right_side):
    return jnp.einsum(einsum_recipe, left_side, right_side, preferred_element_type=jnp.float32)


def per_device(focusing, v_factors, u_factors, tile_ranks, owners, onsets):
    count_col = lax.axis_size("col")
    my_column = lax.axis_index("col")
    count_freq = lax.axis_size("freq")
    my_freq = lax.axis_index("freq")
    freq_dev = focusing.shape[0]
    vis_dev = focusing.shape[2]
    sources_dev = focusing.shape[3]
    capacity = u_factors.shape[2]
    block_width = min(sources_dev, TS)
    blocks_dev = sources_dev // block_width
    per_tile = TS // block_width
    all_blocks = count_col * blocks_dev
    row_tiles = NR // TS
    col_tiles = NS // TS
    freq_all = freq_dev * count_freq
    quarter = TS // count_freq
    tile_ids = jnp.arange(row_tiles, dtype=jnp.int32)
    same_owner = owners[:, None] == owners[None, :]
    earlier = tile_ids[None, :] < tile_ids[:, None]
    slot_of = jnp.sum((same_owner & earlier).astype(jnp.int32), axis=1)
    slot_ids = jnp.arange(capacity, dtype=jnp.int32)
    routing = (owners[None, None, :] == jnp.arange(count_col, dtype=jnp.int32)[:, None, None]) & (
        slot_of[None, None, :] == slot_ids[None, :, None]
    )
    lower_routing = routing.astype(jnp.bfloat16)
    my_slots = ((owners[None, :] == my_column) & (slot_of[None, :] == slot_ids[:, None])).astype(
        jnp.int32
    )
    slot_ranks = jnp.sum(my_slots[:, :, None] * tile_ranks[None, :, :], axis=1)
    rank_mask = (jnp.arange(R, dtype=jnp.int32)[None, None, :] < slot_ranks[:, :, None]).astype(
        jnp.float32
    )
    slot_onsets = jnp.sum(my_slots[:, :, None] * onsets.reshape(row_tiles, TS)[None], axis=1)
    slot_onsets = jnp.maximum(slot_onsets, 1)
    focus_low = focusing.astype(jnp.bfloat16).reshape(freq_dev, 2, vis_dev, blocks_dev, block_width)
    factors_v = v_factors.reshape(freq_dev, 2, row_tiles, R, blocks_dev, block_width)
    einsum_recipe = "fikbs,fvbs->ifbkv"
    real_portion = kernel_product(einsum_recipe, factors_v[:, 0], focus_low[:, 0]) - kernel_product(
        einsum_recipe, factors_v[:, 1], focus_low[:, 1]
    )
    part_imag = kernel_product(einsum_recipe, factors_v[:, 0], focus_low[:, 1]) + kernel_product(
        einsum_recipe, factors_v[:, 1], focus_low[:, 0]
    )
    partial_sums = jnp.stack([real_portion, part_imag], axis=3).astype(jnp.bfloat16)
    outgoing_parts = kernel_product("way,ymleno->amwleno", lower_routing, partial_sums).astype(
        jnp.bfloat16
    )
    outgoing_parts = outgoing_parts.reshape(capacity, freq_dev, all_blocks, 2, R, vis_dev)
    arrived = lax.all_to_all(outgoing_parts, "col", split_axis=2, concat_axis=2, tiled=True)
    coefficients = jnp.sum(
        arrived.astype(jnp.float32).reshape(capacity, freq_dev, col_tiles, per_tile, 2, R, vis_dev),
        axis=3,
    )
    coefficients = (coefficients * rank_mask[:, None, :, None, :, None]).astype(jnp.bfloat16)
    factors_u = u_factors.reshape(freq_dev, 2, capacity, col_tiles, R, TS)
    uform = "fcjka,cfjkv->cfav"
    field_real = kernel_product(uform, factors_u[:, 0], coefficients[:, :, :, 0]) - kernel_product(
        uform, factors_u[:, 1], coefficients[:, :, :, 1]
    )
    field_imag = kernel_product(uform, factors_u[:, 0], coefficients[:, :, :, 1]) + kernel_product(
        uform, factors_u[:, 1], coefficients[:, :, :, 0]
    )
    receiver_field = jnp.stack([field_real, field_imag], axis=2).astype(jnp.bfloat16)
    turned = lax.all_to_all(receiver_field, "freq", split_axis=3, concat_axis=1, tiled=True)
    quarter_onsets = lax.dynamic_slice_in_dim(slot_onsets, my_freq * quarter, quarter, 1)
    mixing = window_tables(freq_all, quarter_onsets.reshape(-1)).reshape(
        capacity, quarter, 2 * freq_all, 2 * freq_all
    )
    flat_field = turned.reshape(capacity, 2 * freq_all, quarter, vis_dev).astype(jnp.float32)
    mixed_field = jnp.einsum("crpq,cqrv->cprv", mixing, flat_field, precision=lax.Precision.HIGHEST)
    mixed_field = mixed_field.astype(jnp.bfloat16).reshape(capacity, freq_all, 2, quarter, vis_dev)
    windowed = lax.all_to_all(mixed_field, "freq", split_axis=1, concat_axis=3, tiled=True)
    aform = "fcjka,cfav->cfjkv"
    back_real = kernel_product(aform, factors_u[:, 0], windowed[:, :, 0]) + kernel_product(
        aform, factors_u[:, 1], windowed[:, :, 1]
    )
    back_imag = kernel_product(aform, factors_u[:, 0], windowed[:, :, 1]) - kernel_product(
        aform, factors_u[:, 1], windowed[:, :, 0]
    )
    adjoint = jnp.stack([back_real, back_imag], axis=3) * rank_mask[:, None, :, None, :, None]
    adjoint = adjoint.astype(jnp.bfloat16)
    spread = jnp.broadcast_to(
        adjoint[:, :, :, None], (capacity, freq_dev, col_tiles, per_tile, 2, R, vis_dev)
    )
    spread = spread.reshape(capacity, freq_dev, all_blocks, 2, R, vis_dev)
    result_field = lax.all_to_all(spread, "col", split_axis=2, concat_axis=2, tiled=True)
    result_field = result_field.reshape(capacity, freq_dev, count_col, blocks_dev, 2, R, vis_dev)
    row_share = kernel_product("prq,rjpagwu->qjagwu", lower_routing, result_field).astype(
        jnp.bfloat16
    )
    wform = "fikbs,ifbkv->fvbs"
    wave_real = kernel_product(wform, factors_v[:, 0], row_share[:, :, :, 0]) + kernel_product(
        wform, factors_v[:, 1], row_share[:, :, :, 1]
    )
    wave_imag = kernel_product(wform, factors_v[:, 0], row_share[:, :, :, 1]) - kernel_product(
        wform, factors_v[:, 1], row_share[:, :, :, 0]
    )
    wave_field = jnp.stack([wave_real, wave_imag], axis=1).reshape(
        freq_dev, 2, vis_dev, sources_dev
    )
    return focusing - wave_field


def window_rows(onset_row, my_freq):
    sign = (2 * my_freq - 1).astype(jnp.float32)

    def sums(bins, inverse):
        phase_all = jnp.bitwise_and(bins * onset_row, 2 * NT - 1).astype(jnp.float32) * (math.pi / NT)
        phase_less = jnp.bitwise_and(bins * (onset_row - 1), 2 * NT - 1).astype(jnp.float32) * (math.pi / NT)
        scaled = jnp.sin(phase_all) * inverse
        return jnp.cos(phase_less) * scaled, jnp.sin(phase_less) * scaled

    def inverse_of(bins):
        return 1.0 / (NT * math.sin(math.pi * bins / NT))

    own_inverse = jnp.where(my_freq == 0, inverse_of(2 * KLO), inverse_of(2 * KLO + 2))
    own_cos, own_sin = sums(2 * KLO + 2 * my_freq, own_inverse)
    sum_cos, sum_sin = sums(2 * KLO + 1, inverse_of(2 * KLO + 1))
    gap_cos, gap_sin = sums(1, inverse_of(1))
    level = onset_row.astype(jnp.float32) * (1.0 / NT)
    real_row = (level + own_cos, -own_sin, gap_cos + sum_cos, sign * gap_sin - sum_sin)
    imag_row = (-own_sin, level - own_cos, -sum_sin - sign * gap_sin, gap_cos - sum_cos)
    return real_row, imag_row


def stacked_dot(left_side, right_side, dims):
    return lax.dot_general(left_side, right_side, (dims, ((), ())), preferred_element_type=jnp.float32)


def fused_kernel(
    count_col,
    owners_ref,
    ranks_ref,
    onsets_ref,
    focus_hbm,
    v_hbm,
    u_hbm,
    focus_buf,
    v_place,
    last_left,
    v_buf,
    u_buf,
    far_u,
    part_buf,
    coef_send,
    coef_recv,
    field_buf,
    window_buf,
    table_buf,
    adj_send,
    adj_recv,
    adj_rows,
    route_buf,
    focus_sem,
    v_sem,
    u_sem,
    coef_send_sem,
    coef_recv_sem,
    adj_send_sem,
    adj_recv_sem,
    far_send_sem,
    far_recv_sem,
):
    my_col = lax.axis_index("col")
    my_freq = lax.axis_index("freq")
    my_grp = lax.axis_index("grp")
    my_rep = lax.axis_index("rep")
    blocks = focus_buf.shape[0]
    vis = focus_buf.shape[2]
    row_tiles = NR // TS
    col_tiles = NS // TS
    band = blocks * R
    ranks_all = row_tiles * R
    ranks_u = col_tiles * R
    strips = TS // LANES
    quarter = ranks_u // 4
    piece = quarter // CHUNKS
    places = 2 * ROUNDS * count_col
    round_rows = 2 * count_col * R
    peers = [(dx, dz) for dz in ORDER for dx in (1, 0) if dx or dz]
    assert len(peers) == 2 * count_col - 1

    def peer_index(dx, dz):
        return dz * 2 + dx - 1

    def place_of(c, freq, col):
        return (c * 2 + freq) * count_col + col

    def focus_copy(b):
        return pltpu.make_async_copy(
            focus_hbm.at[0, :, :, pl.ds(pl.multiple_of(b * TS, TS), TS)], focus_buf.at[b], focus_sem.at[b]
        )

    def v_copy(b):
        return pltpu.make_async_copy(
            v_hbm.at[0, :, :, pl.ds(pl.multiple_of(b * TS, TS), TS)], v_buf.at[b], v_sem.at[b]
        )

    def u_copy(c):
        return pltpu.make_async_copy(u_hbm.at[0, :, 2 * my_freq + c], u_buf.at[c], u_sem.at[c])

    def col_at(dz):
        return lax.rem(my_col + dz, count_col)

    def freq_at(dx):
        return my_freq if dx == 0 else 1 - my_freq

    def device_at(dx, dz):
        return {"freq": freq_at(dx), "col": col_at(dz)}

    def coef_copy(c, dx, dz):
        at = peer_index(dx, dz)
        return pltpu.make_async_remote_copy(
            src_ref=coef_send.at[c, at],
            dst_ref=coef_recv.at[c, my_freq, :, pl.ds(pl.multiple_of(my_col * band, 32), band), :],
            send_sem=coef_send_sem.at[c, at],
            recv_sem=coef_recv_sem.at[c, at],
            device_id=device_at(dx, dz),
            device_id_type=pl.DeviceIdType.MESH,
        )

    def adj_copy(c, dx, dz):
        at = peer_index(dx, dz)
        return pltpu.make_async_remote_copy(
            src_ref=adj_send.at[c, dx, :, pl.ds(pl.multiple_of(col_at(dz) * band, 32), band), :],
            dst_ref=adj_recv.at[place_of(c, my_freq, my_col)],
            send_sem=adj_send_sem.at[c, at],
            recv_sem=adj_recv_sem.at[c, at],
            device_id=device_at(dx, dz),
            device_id_type=pl.DeviceIdType.MESH,
        )

    def far_copy(stage, g):
        c, chunk = divmod(g, CHUNKS)
        grp = 1 - my_grp if stage == 3 else my_grp
        rows = pl.ds(pl.multiple_of((2 * my_rep + grp) * quarter + chunk * piece, 16), piece)
        target = far_u.at[c, :, rows, :]
        source = u_hbm.at[0, :, 2 * (1 - my_freq) + c, rows, :] if stage == 0 else target
        device = ({"freq": 1 - my_freq}, {"grp": 1 - my_grp}, {"rep": 1 - my_rep}, {"rep": 1 - my_rep})[stage]
        return pltpu.make_async_remote_copy(
            src_ref=source,
            dst_ref=target,
            send_sem=far_send_sem.at[stage, g],
            recv_sem=far_recv_sem.at[stage, g],
            device_id=device,
            device_id_type=pl.DeviceIdType.MESH,
        )

    def far_start(c):
        for chunk in range(CHUNKS):
            far_copy(0, c * CHUNKS + chunk).start()

    barrier = pltpu.get_barrier_semaphore()
    for device in [device_at(dx, dz) for dx, dz in peers] + [{"grp": 1 - my_grp}, {"rep": 1 - my_rep}]:
        pl.semaphore_signal(barrier, inc=1, device_id=device, device_id_type=pl.DeviceIdType.MESH)

    for b in range(blocks):
        focus_copy(b).start()
        v_copy(b).start()
    for c in range(ROUNDS):
        u_copy(c).start()

    pl.semaphore_wait(barrier, len(peers) + 2)
    far_start(0)

    dest_of = []
    for tile in range(row_tiles):
        slot = jnp.int32(0)
        for other in range(tile):
            slot = slot + (owners_ref[other] == owners_ref[tile]).astype(jnp.int32)
        dest_of.append(place_of(slot % ROUNDS, slot // ROUNDS, owners_ref[tile]))

    def divided(ids):
        return jnp.right_shift(ids * (-(-65536 // R)), 16)

    column_ids = lax.broadcasted_iota(jnp.int32, (1, ranks_all), 1)
    row_ids = lax.broadcasted_iota(jnp.int32, (places * R, ranks_all), 0)
    column_tile = divided(column_ids)
    column_level = column_ids - column_tile * R
    row_place = divided(row_ids)
    row_level = row_ids - row_place * R
    column_dest = jnp.zeros_like(column_ids)
    for tile in range(row_tiles):
        column_dest = jnp.where(column_tile == tile, dest_of[tile], column_dest)
    routed = (row_place == column_dest) & (row_level == column_level)
    for b in range(blocks):
        column_rank = jnp.zeros_like(column_ids)
        for tile in range(row_tiles):
            column_rank = jnp.where(
                column_tile == tile, ranks_ref[tile, my_col * blocks + b], column_rank
            )
        kept = routed & (row_level < column_rank)
        route_buf[b] = jnp.where(kept, 1.0, 0.0).astype(jnp.bfloat16)

    def partial_step(b, carry):
        focus_copy(b).wait()
        v_copy(b).wait()
        focus_low = focus_buf[b].reshape(2 * vis, TS).astype(jnp.bfloat16)
        products = stacked_dot(v_buf[b].reshape(2 * ranks_all, TS), focus_low, ((1,), (1,)))
        real_part = products[:ranks_all, :vis] - products[ranks_all:, vis:]
        imag_part = products[:ranks_all, vis:] + products[ranks_all:, :vis]
        partials = jnp.concatenate([real_part, imag_part], axis=1).astype(jnp.bfloat16)
        placed = stacked_dot(route_buf[b], partials, ((1,), (0,)))
        part_buf[b, 0] = placed[:, :vis]
        part_buf[b, 1] = placed[:, vis:]
        return carry

    def slot_partials(place, part):
        start = pl.multiple_of(place * R, 8)
        pieces = [part_buf[b, part, pl.ds(start, R), :] for b in range(blocks)]
        return jnp.concatenate(pieces, axis=0).astype(jnp.bfloat16)

    def send_coefs(c, wanted):
        for dx, dz in peers:
            if dx in wanted:
                place = place_of(c, freq_at(dx), col_at(dz))
                for part in range(2):
                    coef_send[c, peer_index(dx, dz), part] = slot_partials(place, part)
                coef_copy(c, dx, dz).start()

    def keep_coefs(c):
        for part in range(2):
            coef_recv[c, my_freq, part, pl.ds(pl.multiple_of(my_col * band, 32), band), :] = slot_partials(
                place_of(c, my_freq, my_col), part
            )

    def await_coefs(c, wanted):
        for dx, dz in peers:
            if dx in wanted:
                coef_copy(c, dx, dz).wait_recv()

    def place_factors(b):
        for part in range(2):
            chosen = stacked_dot(route_buf[b], v_buf[b, part], ((1,), (0,)))
            v_place[b, part] = chosen.astype(jnp.bfloat16)

    def field_of(coef, factors):
        real_coef = coef[0]
        imag_coef = coef[1]
        left_side = jnp.concatenate(
            [
                jnp.concatenate([real_coef, imag_coef], axis=1),
                jnp.concatenate([-imag_coef, real_coef], axis=1),
            ],
            axis=0,
        )
        return stacked_dot(left_side, factors.reshape(2 * ranks_u, TS), ((0,), (0,)))

    def own_field(c):
        u_copy(c).wait()
        field_buf[0] = field_of(coef_recv[c, my_freq], u_buf[c])

    def far_field(c):
        field_buf[1] = field_of(coef_recv[c, 1 - my_freq], far_u[c])

    def window_table(c):
        place = place_of(c, my_freq, my_col)
        onset_row = jnp.ones((strips, LANES), jnp.int32)
        for tile in range(row_tiles):
            held = onsets_ref[tile * strips : (tile + 1) * strips, :]
            onset_row = jnp.where(dest_of[tile] == place, held, onset_row)
        for dx in range(2):
            for part, rows in enumerate(window_rows(onset_row, freq_at(dx))):
                for q in range(4):
                    table_buf[c, dx, part, q] = rows[q]

    def window(c, dx):
        for chunk in range(strips):
            lanes = pl.ds(chunk * LANES, LANES)
            ordered = [
                field_buf[side, part * vis : (part + 1) * vis, lanes] for side in (dx, 1 - dx) for part in range(2)
            ]
            for part in range(2):
                total = table_buf[c, dx, part, 0, chunk : chunk + 1] * ordered[0]
                for q in range(1, 4):
                    total = total + table_buf[c, dx, part, q, chunk : chunk + 1] * ordered[q]
                window_buf[dx, part * vis : (part + 1) * vis, lanes] = total.astype(jnp.bfloat16)

    def adjoint(c, dx):
        factors = (u_buf, far_u)[dx][c].reshape(2 * ranks_u, TS)
        products = stacked_dot(factors, window_buf[dx], ((1,), (1,)))
        adj_send[c, dx, 0] = (products[:ranks_u, :vis] + products[ranks_u:, vis:]).astype(jnp.bfloat16)
        adj_send[c, dx, 1] = (products[:ranks_u, vis:] - products[ranks_u:, :vis]).astype(jnp.bfloat16)
        if dx == 0:
            place = place_of(c, my_freq, my_col)
            for part in range(2):
                adj_recv[place, part] = adj_send[c, 0, part, pl.ds(pl.multiple_of(my_col * band, 32), band), :]

    def send_adjoint(c, dx):
        for px, pz in peers:
            if px == dx:
                adj_copy(c, px, pz).start()

    def finish_early():
        for c in range(ROUNDS):
            for dx, dz in peers:
                coef_copy(c, dx, dz).wait_send()
        for dx, dz in peers:
            adj_copy(0, dx, dz).wait_send()
        for stage in range(4):
            for g in range(ROUNDS * CHUNKS):
                far_copy(stage, g).wait_send()

    def gather_side(c, dx):
        for px, pz in peers:
            if px == dx:
                adj_copy(c, px, pz).wait_recv()
        for col in range(count_col):
            place = place_of(c, freq_at(dx), col)
            start = pl.multiple_of(place * R, 8)
            for part in range(2):
                rows = adj_recv[place, part].astype(jnp.float32)
                for b in range(blocks):
                    adj_rows[b, pl.ds(start, R), part * vis : (part + 1) * vis] = rows[b * R : (b + 1) * R]

    def left_of(rows):
        real_adj = rows[:, :vis].astype(jnp.bfloat16)
        imag_adj = rows[:, vis:].astype(jnp.bfloat16)
        return jnp.concatenate(
            [
                jnp.concatenate([real_adj, imag_adj], axis=1),
                jnp.concatenate([imag_adj, -real_adj], axis=1),
            ],
            axis=0,
        )

    def wave_of(b, start, count):
        held = pl.ds(start if isinstance(start, int) else pl.multiple_of(start, 32), count)
        factors = v_place[b, :, held, :].reshape(2 * count, TS)
        return stacked_dot(left_of(adj_rows[b, held, :]), factors, ((0,), (0,))).reshape(2, vis, TS)

    def round_update(b, carry):
        focus_buf[b] = focus_buf[b] - wave_of(b, 0, round_rows)
        return carry

    def side_rows(dx):
        return place_of(1, freq_at(dx), 0) * R

    def side_update(dx):
        def update(b, carry):
            focus_buf[b] = focus_buf[b] - wave_of(b, side_rows(dx), round_rows // 2)
            return carry

        lax.fori_loop(0, blocks, update, 0)

    def hand_over(dx):
        held = pl.ds(pl.multiple_of(side_rows(dx), 32), round_rows // 2)
        for b in range(blocks):
            last_left[b] = left_of(adj_rows[b, held, :])

    def from_freq(g):
        far_copy(0, g).wait_recv()
        far_copy(1, g).start()
        far_copy(2, g).start()

    def from_grp(g):
        far_copy(1, g).wait_recv()
        far_copy(3, g).start()

    def await_far(c):
        for g in range(c * CHUNKS, (c + 1) * CHUNKS):
            far_copy(2, g).wait_recv()
            far_copy(3, g).wait_recv()

    partial_step(0, 0)
    lax.fori_loop(1, blocks, partial_step, 0)
    send_coefs(0, (1,))
    far_start(1)
    send_coefs(0, (0,))
    send_coefs(1, (0,))
    from_freq(0)
    keep_coefs(0)
    keep_coefs(1)
    place_factors(0)
    window_table(0)
    from_freq(1)
    from_grp(0)
    place_factors(1)
    window_table(1)
    from_freq(2)
    from_grp(1)
    await_coefs(0, (0,))
    own_field(0)
    from_grp(2)
    from_freq(3)
    await_coefs(0, (1,))
    await_far(0)
    far_field(0)
    send_coefs(1, (1,))
    window(0, 0)
    adjoint(0, 0)
    send_adjoint(0, 0)
    from_freq(4)
    from_grp(3)
    window(0, 1)
    adjoint(0, 1)
    place_factors(2)
    place_factors(3)
    from_freq(5)
    from_grp(4)
    send_adjoint(0, 1)
    await_coefs(1, (0,))
    own_field(1)
    from_grp(5)
    await_coefs(1, (1,))
    await_far(1)
    far_field(1)
    window(1, 1)
    adjoint(1, 1)
    send_adjoint(1, 1)
    window(1, 0)
    adjoint(1, 0)
    send_adjoint(1, 0)
    gather_side(0, 0)
    gather_side(0, 1)
    lax.fori_loop(0, blocks, round_update, 0)
    finish_early()
    gather_side(1, 1)
    side_update(1)
    gather_side(1, 0)
    hand_over(0)

    for dx, dz in peers:
        adj_copy(1, dx, dz).wait_send()


def last_kernel(focus_ref, factors_ref, left_ref, out_hbm, out_buf, out_sem):
    blocks = focus_ref.shape[0]
    count = left_ref.shape[1] // 2
    vis = focus_ref.shape[2]
    start = pl.multiple_of((2 + lax.axis_index("freq")) * count, 32)

    def out_copy(b, part):
        return pltpu.make_async_copy(
            out_buf.at[b, part], out_hbm.at[0, part, :, pl.ds(b * TS, TS)], out_sem.at[b, part]
        )

    for b in range(blocks):
        factors = factors_ref[b, :, pl.ds(start, count), :].reshape(2 * count, TS)
        for part in range(2):
            wave = stacked_dot(left_ref[b, :, part * vis : (part + 1) * vis], factors, ((0,), (0,)))
            out_buf[b, part] = focus_ref[b, part] - wave
            out_copy(b, part).start()
    for b in range(blocks):
        for part in range(2):
            out_copy(b, part).wait()


def fused_device(focusing, v_factors, u_factors, tile_ranks, owners, onsets):
    count_col = lax.axis_size("col")
    vis = focusing.shape[2]
    sources_dev = focusing.shape[3]
    blocks = sources_dev // TS
    ranks_all = (NR // TS) * R
    ranks_u = (NS // TS) * R
    band = blocks * R
    low = jnp.bfloat16
    peers = 2 * count_col - 1
    places = 2 * ROUNDS * count_col
    dma = pltpu.SemaphoreType.DMA
    scratch = [
        pltpu.VMEM((blocks, 2, ranks_all, TS), low),
        pltpu.VMEM((ROUNDS, 2, ranks_u, TS), low),
        pltpu.VMEM((ROUNDS, 2, ranks_u, TS), low),
        pltpu.VMEM((blocks, 2, places * R, vis), jnp.float32),
        pltpu.VMEM((ROUNDS, peers, 2, band, vis), low),
        pltpu.VMEM((ROUNDS, 2, 2, ranks_u, vis), low),
        pltpu.VMEM((2, 2 * vis, TS), jnp.float32),
        pltpu.VMEM((2, 2 * vis, TS), low),
        pltpu.VMEM((ROUNDS, 2, 2, 4, TS // LANES, LANES), jnp.float32),
        pltpu.VMEM((ROUNDS, 2, 2, ranks_u, vis), low),
        pltpu.VMEM((places, 2, band, vis), low),
        pltpu.VMEM((blocks, places * R, 2 * vis), jnp.float32),
        pltpu.VMEM((blocks, places * R, ranks_all), low),
        dma((blocks,)),
        dma((blocks,)),
        dma((ROUNDS,)),
        dma((ROUNDS, peers)),
        dma((ROUNDS, peers)),
        dma((ROUNDS, peers)),
        dma((ROUNDS, peers)),
        dma((4, ROUNDS * CHUNKS)),
        dma((4, ROUNDS * CHUNKS)),
    ]
    handed = [
        pltpu.VMEM((blocks, 2, vis, TS), jnp.float32),
        pltpu.VMEM((blocks, 2, places * R, TS), low),
        pltpu.VMEM((blocks, 2 * count_col * R, 2 * vis), low),
    ]
    held = pl.BlockSpec(memory_space=pltpu.VMEM)
    passed = pl.pallas_call(
        functools.partial(fused_kernel, count_col),
        out_shape=handed,
        in_specs=[
            pl.BlockSpec(memory_space=pltpu.SMEM),
            pl.BlockSpec(memory_space=pltpu.SMEM),
            pl.BlockSpec(memory_space=pltpu.VMEM),
            pl.BlockSpec(memory_space=pl.ANY),
            pl.BlockSpec(memory_space=pl.ANY),
            pl.BlockSpec(memory_space=pl.ANY),
        ],
        out_specs=[held] * 3,
        scratch_shapes=scratch,
        compiler_params=pltpu.CompilerParams(
            collective_id=0, has_side_effects=True, vmem_limit_bytes=FIRST_VMEM * 1024 * 1024
        ),
        name="marchenko",
    )(owners, tile_ranks, onsets.reshape(NR // LANES, LANES), focusing, v_factors, u_factors)
    return pl.pallas_call(
        last_kernel,
        out_shape=jax.ShapeDtypeStruct(focusing.shape, jnp.float32),
        in_specs=[held] * 3,
        out_specs=pl.BlockSpec(memory_space=pl.ANY),
        scratch_shapes=[pltpu.VMEM((blocks, 2, vis, TS), jnp.float32), dma((blocks, 2))],
        compiler_params=pltpu.CompilerParams(vmem_limit_bytes=8 * 1024 * 1024),
        name="last_update",
    )(*passed)


def choose(focusing, v_factors, u_factors, tile_ranks, owners, onsets):
    whole_blocks = focusing.shape[3] % TS == 0
    paired = lax.axis_size("freq") == 2 and focusing.shape[0] == 1
    replicas = lax.axis_size("grp") == 2 and lax.axis_size("rep") == 2
    slots = u_factors.shape[2] == 2 * ROUNDS and lax.axis_size("col") == 4
    program = fused_device if whole_blocks and paired and replicas and slots else per_device
    return program(focusing, v_factors, u_factors, tile_ranks, owners, onsets)


def solution(mesh):
    return jax.shard_map(
        choose,
        mesh=mesh,
        in_specs=(
            P("freq", None, ("grp", "rep"), "col"),
            P("freq", None, None, "col"),
            P("freq", None, "col", None, None),
            P(),
            P(),
            P(),
        ),
        out_specs=P("freq", None, ("grp", "rep"), "col"),
        check_vma=False,
    )
```
